32 devices in a mesh: seq: 4 (over z), head: 8 (over y, x, core).
Axes of the slice: x: 2, y: 2, z: 4, core: 2. Of those that a mesh axis runs over, the one named last changes fastest.
Arguments:
- inputs: bfloat16 [2048, 8192], P('seq'), may hold values from -6 to 6
- w_qkv: bfloat16 [3, 8192, 2048], P(None, None, 'head'), may hold values from -0.0625 to 0.0625
- w_out: bfloat16 [2048, 8192], P('head'), may hold values from -0.1875 to 0.1875
- turn_ids: int32 [4, 512], P('seq'), may hold values from 0 to 15, never falling along the last dimension, each value on 1 to 64 neighbouring positions
- picked: int32 [4, 64], P('seq'), may hold values from 0 to 511
- owners: int32 [256, 1], P('seq'), may hold values from 0 to 7; in each aligned block of 64 rows (0 to 63, 64 to 127, ...) at most 32 rows name the same one
- candidates: bfloat16 [2048, 8192], P(('seq', 'head')), may hold values from -0.25 to 0.25
Outputs:
- mixed: bfloat16 [2048, 8192], P('seq', 'head')
- scores: float32 [1024, 64], P(('seq', 'head'))
The draws below stay inside these ranges and needn't reach their ends.
Inputs may be any that keep to these rules, and one draw needn't show every extreme that they name: `turn_ids`: within each session turn numbers start at 0, never fall, and each turn has 1 to 64 tokens. `owners`: among the 64 picked rows of one session no owner is named more than 32 times.
All inputs are finite; a program needn't handle non-finite values.
Results may differ from the reference program's by a relative error of at most 0.008.
Values may be sent and summed in bfloat16 or wider, within the bound.
No kernel may reach another device: no remote copies, remote signals or barrier semaphores. Data moves between devices by JAX's collectives and lax.ppermute only.
A program may use at most 128 MiB of HBM per device.

```python
import math
import jax
import jax.numpy as jnp
import numpy as np
from jax import lax

D = 8192
HDIM = 128
HEADS = 16
TOK_DEV = 512
TOKENS = 2048
TURNS = 16
TURN_MOST = 64
R_DEV = 64
SEL = 256
CAP = 32
NC = 64
CANDS = 2048
N_SEQ = 4
N_HEAD = 8


def plant(values, own_key, least, largest):
    extent = values.shape
    index_at = [jax.random.randint(jax.random.fold_in(own_key, axis), (), 0, extent[axis]) for axis in range(len(extent))]
    values = values.at[tuple(index_at)].set(least)
    longest = extent.index(max(extent))
    index_at[longest] = (index_at[longest] + 1) % extent[longest]
    return values.at[tuple(index_at)].set(largest)


def raised(result, own_key, source, target, parts, factor):
    owner, partner = [(jnp.arange(result.shape[axis_at]) // (result.shape[axis_at] // parts)).reshape([-1 if axis == axis_at else 1 for axis in range(result.ndim)]) for axis_at in (source, target)]
    chosen = jax.random.permutation(own_key, parts)[partner]
    strong = (owner == chosen) | (owner == (partner + parts // 2) % parts)
    return jnp.where(strong, factor * result, result)


def steps_of(stream_key, dims, cuts, least, top_value):
    def one(position, blocks):
        heights = jax.random.uniform(jax.random.fold_in(jax.random.fold_in(stream_key, 6), position), (blocks,), jnp.float32, least / len(cuts), top_value / len(cuts))
        return jnp.repeat(jnp.exp(heights), dims[position] // blocks).reshape((-1,) + (1,) * (len(dims) - position - 1))

    level = one(*cuts[0])
    for cut in cuts[1:]:
        level = level * one(*cut)
    return level


def length_profile(amount, total, reach, lean):
    weights = [(1 << 20) // math.isqrt(standing ** lean) + 1 for standing in range(2, amount + 1)]
    spare, counts = total - reach - (amount - 1), [1] * (amount - 1)
    while spare > 0:
        free = [i for i in range(amount - 1) if counts[i] < reach]
        pool, left = sum([weights[i] for i in free]), spare
        for i in free:
            addition = min(reach - counts[i], max(1, left * weights[i] // pool), spare)
            counts[i] = counts[i] + addition
            spare = spare - addition
    return np.array([reach] + counts)


def ragged_sizes(own_key, amount, total, most, slope):
    if amount == 2:
        one = jax.random.randint(own_key, (), max(1, total - most), min(most, total - 1) + 1)
        return jnp.stack([one, total - one])
    lengths = jnp.asarray(length_profile(amount, total, most, slope), jnp.int32)
    pairs = (amount - 1) // 2
    source_of, receiver = lengths[1:1 + 2 * pairs:2], lengths[2:2 + 2 * pairs:2]
    room = jnp.minimum(source_of - 1, most - receiver)
    passed = jax.random.randint(jax.random.fold_in(own_key, 1), (pairs,), 0, 1 << 20) % (room + 1)
    lengths = lengths.at[1:1 + 2 * pairs:2].set(source_of - passed).at[2:2 + 2 * pairs:2].set(receiver + passed)
    return lengths[jax.random.permutation(jax.random.fold_in(own_key, 2), amount)]


def routed_block(key, own, number, rows, number_of, top, limit, lean):
    sequence = jax.random.permutation(key, number_of)
    crowded, ordinary = portions_of(number_of, rows * top, limit, lean, True), portions_of(number_of, rows * top, limit, lean, False)
    places = jnp.arange(number_of)

    def named(sizes, turn):
        used = int((sizes > 0).sum())
        fixed = max(1, used // 4)
        shifted = fixed + (places - fixed + turn * (used - fixed)) % max(1, number_of - fixed)
        return jnp.zeros((number_of,), jnp.int32).at[sequence[jnp.where(places < fixed, places, shifted)]].set(jnp.asarray(sizes, jnp.int32))

    sizes = jnp.where(number % 4 == 0, named(crowded, number // 4), named(ordinary, number - number // 4 - 1))
    mixed = jax.random.permutation(jax.random.fold_in(own, 3), number_of)
    source_of, receiver = mixed[0:number_of // 2 * 2:2], mixed[1:number_of // 2 * 2:2]
    margin = jnp.minimum(sizes[source_of] - 1, limit - sizes[receiver]) // 2
    margin = jnp.where((source_of == sequence[0]) | (receiver == sequence[0]) | (sizes[receiver] == 0), 0, jnp.maximum(margin, 0))
    shifted = jax.random.randint(jax.random.fold_in(own, 4), (number_of // 2,), 0, 1 << 20) % (margin + 1)
    sizes = sizes.at[source_of].add(-shifted).at[receiver].add(shifted)
    labels = jnp.searchsorted(jnp.cumsum(sizes), jnp.arange(rows * top), side="right").astype(jnp.int32)
    listing = labels.reshape(top, rows).T
    listing = listing[jax.random.permutation(jax.random.fold_in(own, 1), rows)]
    turn = jax.random.randint(jax.random.fold_in(own, 2), (rows, 1), 0, top)
    return jnp.take_along_axis(listing, (jnp.arange(top)[None, :] + turn) % top, axis=1)


def portions_of(amount, total, reach, skew, full):
    weights = [(1 << 20) // math.isqrt(grade ** skew) + 1 for grade in range(1, amount + 1)]
    largest = reach if full else min(reach, max(-(-total // amount), total * weights[0] // sum(weights)))
    least = 1 if total - largest >= amount - 1 else 0
    holding, spare = [largest] + [least] * (amount - 1), total - largest - least * (amount - 1)
    while spare > 0:
        free = [i for i in range(1, amount) if holding[i] < largest] or [i for i in range(1, amount) if holding[i] < reach]
        pool, left = sum([weights[i] for i in free]), spare
        for i in free:
            addition = min(reach - holding[i], max(1, left * weights[i] // pool), spare)
            holding[i] = holding[i] + addition
            spare = spare - addition
    return np.array(holding)


def centred(own_key, extent, deviation, bound, cuts=(), held_as=jnp.bfloat16):
    result = jax.random.normal(own_key, extent, jnp.float32) * deviation
    if len(cuts) > 0:
        result = steps_of(own_key, extent, cuts, -0.22, 0.18) * result
    return jnp.clip(result, min=-bound, max=bound).astype(held_as)


def gaussian_with(own_key, dims, width, most, cuts, heavy, kind=jnp.bfloat16):
    result = width * jax.random.normal(own_key, dims, jnp.float32)
    if cuts:
        result = result * steps_of(own_key, dims, cuts, -0.22, 0.18)
    return jnp.clip(raised(result, jax.random.fold_in(own_key, 3), *heavy), -most, most).astype(kind)


def setup_inputs(seed: int = 0) -> dict:
    streams_of = jax.random.split(jax.random.key(seed), 8)
    inputs = centred(streams_of[0], (TOKENS, D), 1.0, 6.0, ((0, 4),))
    w_qkv = centred(streams_of[1], (3, D, HEADS * HDIM), D ** -0.5, 0.0625, ((2, 8),))
    w_out = gaussian_with(streams_of[2], (HEADS * HDIM, D), (HEADS * HDIM) ** -0.5, 0.1875, ((0, 8),), (0, 1, 8, 2.0))
    turn_ids = jax.vmap(lambda own: jnp.searchsorted(jnp.cumsum(ragged_sizes(own, TURNS, TOK_DEV, TURN_MOST, 2)), jnp.arange(TOK_DEV), side="right"))(jax.random.split(streams_of[3], N_SEQ)).reshape((N_SEQ, TOK_DEV)).astype(jnp.int32)
    picked = plant(jax.random.randint(streams_of[4], (N_SEQ, R_DEV), 0, TOK_DEV), jax.random.fold_in(streams_of[4], 1), 0, TOK_DEV - 1).astype(jnp.int32)
    owners_keys = jax.random.split(jax.random.fold_in(streams_of[5], 1), SEL // R_DEV)
    owners_turns = jax.random.permutation(jax.random.fold_in(streams_of[5], 3), SEL // R_DEV)
    owners = jax.vmap(lambda own, number: routed_block(jax.random.fold_in(streams_of[5], 2), own, number, R_DEV, N_HEAD, 1, CAP, 2))(owners_keys, owners_turns).reshape((SEL, 1))
    candidates = centred(streams_of[6], (CANDS, D), (D // 16) ** -0.5, 0.25, ((0, 32),))
    return dict(inputs=inputs, w_qkv=w_qkv, w_out=w_out, turn_ids=turn_ids, picked=picked, owners=owners, candidates=candidates)


def session_block(operands):
    q_block, k_block, v_block, pre_state = operands
    raw_scores = jnp.einsum('thi,shi->hts', q_block.astype(jnp.float32), k_block.astype(jnp.float32))
    tok_pos = jnp.arange(q_block.shape[0], dtype=jnp.int32)
    causal = tok_pos[:, None] >= tok_pos[None, :]
    weights = jnp.where(causal[None, :, :], raw_scores, 0.0).astype(jnp.bfloat16)
    local_part = jnp.einsum('hts,shj->thj', weights.astype(jnp.float32), v_block.astype(jnp.float32))
    carried = jnp.einsum('thi,hij->thj', q_block.astype(jnp.float32), pre_state.astype(jnp.float32))
    summed = local_part + carried
    normed = summed * lax.rsqrt(lax.optimization_barrier(jnp.mean(summed * summed, axis=-1, keepdims=True)) + 1e-05)
    return normed.astype(jnp.bfloat16)

def reference(inputs, w_qkv, w_out, turn_ids, picked, owners, candidates):
    n_seq = turn_ids.shape[0]
    tok_dev = turn_ids.shape[1]
    head_count = w_qkv.shape[2] // HDIM
    projected = []
    for proj_index in range(3):
        projected.append(jnp.dot(inputs, w_qkv[proj_index], preferred_element_type=jnp.float32).astype(jnp.bfloat16))
    query = projected[0].reshape(n_seq, tok_dev, head_count, HDIM)
    keys = projected[1].reshape(n_seq, tok_dev, head_count, HDIM)
    values = projected[2].reshape(n_seq, tok_dev, head_count, HDIM)
    states = jnp.einsum('bthi,bthj->bhij', keys.astype(jnp.float32), values.astype(jnp.float32))
    zero_state = jnp.zeros((1,) + states.shape[1:], jnp.float32)
    prefix = jnp.cumsum(jnp.concatenate([zero_state, states[:-1]], axis=0), axis=0).astype(jnp.bfloat16)
    attended = lax.map(session_block, (query, keys, values, prefix))
    attended = attended.reshape(n_seq * tok_dev, head_count * HDIM)
    mixed_sum = inputs.astype(jnp.float32) + jnp.dot(attended, w_out, preferred_element_type=jnp.float32)
    mixed = mixed_sum.astype(jnp.bfloat16)
    mixed_rows = mixed.reshape(n_seq, tok_dev, mixed.shape[1])
    r_dev = picked.shape[1]
    n_head = candidates.shape[0] // (NC * n_seq)
    cap_rows = 4 * r_dev // n_head
    owner_rows = owners[:, 0].reshape(n_seq, r_dev)
    cand_rows = candidates.reshape(n_seq, n_head, NC, candidates.shape[1])
    tok_pos = jnp.arange(tok_dev, dtype=jnp.int32)
    row_pos = jnp.arange(r_dev, dtype=jnp.int32)
    head_pos = jnp.arange(n_head, dtype=jnp.int32)
    results = []
    for session in range(n_seq):
        turn_row = turn_ids[session]
        pick_row = picked[session]
        pick_hot = tok_pos[None, :] == pick_row[:, None]
        sel_turn = lax.optimization_barrier(jnp.sum(jnp.where(pick_hot, turn_row[None, :], 0), axis=1)).astype(jnp.int32)
        member = (turn_row[None, :] == sel_turn[:, None]) & (tok_pos[None, :] <= pick_row[:, None])
        row_count = lax.optimization_barrier(jnp.sum(member.astype(jnp.float32), axis=1))
        pooled = jnp.dot(member.astype(jnp.bfloat16), mixed_rows[session], preferred_element_type=jnp.float32)
        summary = (pooled / row_count[:, None]).astype(jnp.bfloat16)
        owner_row = owner_rows[session]
        own_hot = (owner_row[:, None] == head_pos[None, :]).astype(jnp.int32)
        before = (row_pos[:, None] > row_pos[None, :]).astype(jnp.int32)
        slot_rank = lax.optimization_barrier(jnp.sum(jnp.dot(before, own_hot) * own_hot, axis=1)).astype(jnp.int32)
        slot_index = owner_row * cap_rows + slot_rank
        buffer = jnp.zeros((n_head * cap_rows, summary.shape[1]), jnp.bfloat16).at[slot_index].set(summary)
        buffer = buffer.reshape(n_head, cap_rows, summary.shape[1])
        slot_scores = jnp.einsum('okd,ond->okn', buffer.astype(jnp.float32), cand_rows[session].astype(jnp.float32))
        results.append(slot_scores.reshape(n_head * cap_rows, NC))
    scores = jnp.concatenate(results, axis=0)
    return (mixed, scores)
```

```python
import jax
import jax.numpy as jnp
from jax import lax
from jax.sharding import PartitionSpec as P

HDIM = 128
F32 = jnp.float32
BF16 = jnp.bfloat16


def swap(value, mask):
    n = lax.axis_size("head")
    return lax.ppermute(value, "head", [(i, i ^ mask) for i in range(n)])


def per_device(inputs, w_qkv, w_out, turn_ids, picked, owners, candidates):
    tokens_here, model_width = inputs.shape
    heads_here = w_qkv.shape[2] // HDIM
    n_head = lax.axis_size("head")
    n_seq = lax.axis_size("seq")
    chips = n_head // 2
    head = lax.axis_index("head")
    chip, core = lax.shift_right_logical(head, 1), lax.bitwise_and(head, 1)
    cols = model_width // n_head
    wide = 2 * cols

    w_parts = []
    for j in range(chips):
        part = lax.dynamic_slice_in_dim(w_out, (chip ^ j) * wide, wide, 1)
        w_parts.append(part if j == 0 else swap(part, 2 * j))

    keys = jnp.dot(inputs, w_qkv[1], preferred_element_type=F32).astype(BF16)
    values = jnp.dot(inputs, w_qkv[2], preferred_element_type=F32).astype(BF16)
    keys = keys.reshape(tokens_here, heads_here, HDIM)
    values = values.reshape(tokens_here, heads_here, HDIM)
    states = jnp.einsum("thi,thj->hij", keys, values, preferred_element_type=F32)
    states = states.astype(BF16)
    earlier = [
        lax.ppermute(states, "seq", [(i, i + s) for i in range(n_seq - s)])
        for s in range(1, n_seq)
    ]
    query = jnp.dot(inputs, w_qkv[0], preferred_element_type=F32).astype(BF16)
    query = query.reshape(tokens_here, heads_here, HDIM)
    scores_local = jnp.einsum("thi,shi->hts", query, keys, preferred_element_type=F32)
    tok_pos = jnp.arange(tokens_here, dtype=jnp.int32)
    causal = tok_pos[:, None] >= tok_pos[None, :]
    weights = jnp.where(causal[None, :, :], scores_local, 0.0).astype(BF16)
    local_part = jnp.einsum("hts,shj->thj", weights, values, preferred_element_type=F32)
    prefix = sum(e.astype(F32) for e in earlier).astype(BF16)
    carried = jnp.einsum("thi,hij->thj", query, prefix, preferred_element_type=F32)
    summed = local_part + carried
    normed = summed * lax.rsqrt(jnp.mean(summed * summed, axis=-1, keepdims=True) + 1e-05)
    attended = normed.astype(BF16).reshape(tokens_here, heads_here * HDIM)

    attn = [attended] + [swap(attended, 2 * j) for j in range(1, chips)]

    turn_row = turn_ids[0]
    pick_row = picked[0]
    r_dev = pick_row.shape[0]
    cap_rows = 4 * r_dev // n_head
    pick_hot = tok_pos[None, :] == pick_row[:, None]
    sel_turn = jnp.sum(jnp.where(pick_hot, turn_row[None, :], 0), axis=1)
    member = (turn_row[None, :] == sel_turn[:, None]) & (tok_pos[None, :] <= pick_row[:, None])
    row_count = jnp.sum(member.astype(F32), axis=1)
    member = member.astype(BF16)
    chip_inputs = lax.dynamic_slice_in_dim(inputs, chip * wide, wide, 1)
    pooled_in = jnp.dot(member, chip_inputs, preferred_element_type=F32)

    owner_row = owners[:, 0]
    row_pos = jnp.arange(r_dev, dtype=jnp.int32)
    head_pos = jnp.arange(n_head, dtype=jnp.int32)
    own_hot = (owner_row[:, None] == head_pos[None, :]).astype(jnp.int32)
    before = (row_pos[:, None] > row_pos[None, :]).astype(jnp.int32)
    slot_rank = jnp.sum(jnp.dot(before, own_hot) * own_hot, axis=1)

    part_sum = 0.0
    for a, w in zip(attn, w_parts):
        pooled = jnp.dot(member, a, preferred_element_type=F32).astype(BF16)
        part_sum = part_sum + jnp.dot(pooled, w, preferred_element_type=F32)
    summary = ((pooled_in + part_sum + swap(part_sum, 1)) / row_count[:, None]).astype(BF16)

    slots = jnp.arange(cap_rows, dtype=jnp.int32)
    scores = 0.0
    for j in range(chips):
        place = (owner_row == 2 * (chip ^ j) + core)[None, :] & (slot_rank[None, :] == slots[:, None])
        rows = jnp.dot(place.astype(BF16), summary, preferred_element_type=F32).astype(BF16)
        if j:
            rows = swap(rows, 2 * j)
        cand = lax.dynamic_slice_in_dim(candidates, (chip ^ j) * wide, wide, 1)
        scores = scores + lax.dot_general(
            rows, cand, (((1,), (1,)), ((), ())), preferred_element_type=F32
        )

    def columns(at):
        total = 0.0
        for a, w in zip(attn, w_parts):
            w_half = lax.dynamic_slice_in_dim(w, at * cols, cols, 1)
            total = total + jnp.dot(a, w_half, preferred_element_type=F32)
        return total

    other = swap(columns(1 - core).astype(BF16), 1)
    input_cols = lax.dynamic_slice_in_dim(inputs, head * cols, cols, 1)
    mixed = (input_cols.astype(F32) + columns(core) + other.astype(F32)).astype(BF16)
    return (mixed, scores)


def solution(mesh):
    return jax.shard_map(
        per_device,
        mesh=mesh,
        in_specs=(
            P("seq", None),
            P(None, None, "head"),
            P("head", None),
            P("seq", None),
            P("seq", None),
            P("seq", None),
            P(("seq", "head"), None),
        ),
        out_specs=(P("seq", "head"), P(("seq", "head"), None)),
        check_vma=False,
    )
```

```python
import functools
import jax
import jax.numpy as jnp
from jax import lax
from jax.experimental import pallas as pl
from jax.experimental.pallas import tpu as pltpu
from jax.sharding import PartitionSpec as P


HDIM = 128
F32 = jnp.float32
BF16 = jnp.bfloat16
VMEM = pl.BlockSpec(memory_space=pltpu.VMEM)
HBM = pl.BlockSpec(memory_space=pltpu.HBM)
ANY = pl.BlockSpec(memory_space=pl.ANY)


def move(value, masks):
    n = lax.axis_size("head")
    return lax.ppermute(value, "head", [(i, i ^ masks[i % 2]) for i in range(n)])


def dot(a, b):
    return jnp.dot(a, b, preferred_element_type=F32)


def masks_of(half_bits, m):
    return (m << 1, m << (1 + half_bits))


def place(half_bits, m, r):
    head = lax.axis_index("head")
    a, c = masks_of(half_bits, m), masks_of(half_bits, r)[::-1]
    return head ^ jnp.where(lax.bitwise_and(head, 1) == 0, a[0] ^ c[0], a[1] ^ c[1])


def block_of(index, size):
    return pl.ds(pl.multiple_of(index * size, size), size)


def kv_kernel(x_ref, w_ref, k_ref, v_ref, s_ref, x_buf, w_buf, acc, sems, *, steps):
    depth = x_ref.shape[1] // steps
    copies = []
    for s in range(steps):
        at = pl.ds(s * depth, depth)
        copies.append(
            [pltpu.make_async_copy(x_ref.at[:, at], x_buf.at[:, at], sems.at[0, s])]
            + [
                pltpu.make_async_copy(w_ref.at[1 + i, at], w_buf.at[i, at], sems.at[1 + i, s])
                for i in range(2)
            ]
        )
        for copy in copies[-1]:
            copy.start()
    for s in range(steps):
        for copy in copies[s]:
            copy.wait()
        at = pl.ds(s * depth, depth)
        for i in range(2):
            part = dot(x_buf[:, at], w_buf[i, at])
            acc[i] = part if s == 0 else acc[i] + part
    k_ref[...] = acc[0].astype(BF16)
    v_ref[...] = acc[1].astype(BF16)
    for h in range(k_ref.shape[1] // HDIM):
        of = pl.ds(h * HDIM, HDIM)
        state = lax.dot_general(
            k_ref[:, of], v_ref[:, of], (((0,), (0,)), ((), ())), preferred_element_type=F32
        )
        s_ref[h] = state.astype(BF16)


def q_kernel(x_ref, w_ref, k_ref, v_ref, q_ref, l_ref, w_buf, acc, sems, *, steps):
    depth = x_ref.shape[1] // steps
    copies = []
    for s in range(steps):
        at = pl.ds(s * depth, depth)
        copies.append(pltpu.make_async_copy(w_ref.at[0, at], w_buf.at[at], sems.at[s]))
        copies[-1].start()
    for s in range(steps):
        copies[s].wait()
        at = pl.ds(s * depth, depth)
        part = dot(x_ref[:, at], w_buf[at])
        acc[...] = part if s == 0 else acc[...] + part
    q_ref[...] = acc[...].astype(BF16)
    rows = q_ref.shape[0]
    block = min(rows, 256)
    for h in range(q_ref.shape[1] // HDIM):
        of = pl.ds(h * HDIM, HDIM)
        for b in range(0, rows, block):
            seen = b + block
            sc = lax.dot_general(
                q_ref[pl.ds(b, block), of],
                k_ref[pl.ds(0, seen), of],
                (((1,), (1,)), ((), ())),
                preferred_element_type=F32,
            )
            t = lax.broadcasted_iota(jnp.int32, sc.shape, 0) + b
            s = lax.broadcasted_iota(jnp.int32, sc.shape, 1)
            sc = jnp.where(t >= s, sc, 0.0).astype(BF16)
            l_ref[pl.ds(b, block), of] = dot(sc, v_ref[pl.ds(0, seen), of])


def attend_kernel(*refs, others):
    q_ref, l_ref, m_ref = refs[:3]
    states, out_ref = refs[3 : 3 + others], refs[3 + others]
    rows = q_ref.shape[0]
    seq = lax.axis_index("seq")
    for h in range(q_ref.shape[1] // HDIM):
        of = pl.ds(h * HDIM, HDIM)
        prefix = jnp.zeros((HDIM, HDIM), F32)
        for i, state in enumerate(states):
            prefix = prefix + jnp.where((seq ^ (i + 1)) < seq, state[h].astype(F32), 0.0)
        summed = l_ref[:, of] + dot(q_ref[:, of], prefix.astype(BF16))
        scale = lax.rsqrt(jnp.mean(summed * summed, axis=-1, keepdims=True) + 1e-05)
        attn = (summed * scale).astype(BF16)
        out_ref[pl.ds(0, rows), of] = attn
        out_ref[pl.ds(rows, m_ref.shape[0]), of] = dot(m_ref[...], attn).astype(BF16)


def stay(x):
    return pltpu.with_memory_space_constraint(x, pltpu.HBM)


def cut_kernel(w_ref, out_ref, sems, *, m, half_bits):
    count = 1 << half_bits
    cols = out_ref.shape[1] // count
    copies = [
        pltpu.make_async_copy(
            w_ref.at[:, block_of(place(half_bits, m, r), cols)],
            out_ref.at[:, pl.ds(r * cols, cols)],
            sems.at[r],
        )
        for r in range(count)
    ]
    for copy in copies:
        copy.start()
    for copy in copies:
        copy.wait()


def here_kernel(own_ref, peer_ref, m_ref, x_ref, w_ref, wp_ref, out_ref, x_buf, w_buf, sems, *, half_bits):
    side = 1 << half_bits
    cols = out_ref.shape[2]
    rows = m_ref.shape[1]
    order = list(range(1, side)) + [0]
    copies = {}
    for r in order:
        at = block_of(place(half_bits, 0, r), cols)
        for i, ref in enumerate((w_ref, wp_ref)):
            copies[r, i] = pltpu.make_async_copy(ref.at[:, at], w_buf.at[r, i], sems.at[r, i])
            copies[r, i].start()
    own = pltpu.make_async_copy(
        x_ref.at[:, block_of(lax.axis_index("head"), cols)], x_buf, sems.at[side, 0]
    )
    own.start()
    for r in order:
        total = None
        for i, ext in enumerate((own_ref, peer_ref)):
            copies[r, i].wait()
            part = dot(ext[...], w_buf[r, i])
            total = part if total is None else total + part
        out_ref[r] = total
    own.wait()
    out_ref[0, pl.ds(0, rows)] += x_buf[...].astype(F32)
    out_ref[0, pl.ds(rows, m_ref.shape[0])] += dot(m_ref[...], x_buf[...])


def add_kernel(*refs, count, r, rows):
    ext, w, base = refs[:count], refs[count : 2 * count], refs[2 * count]
    r_ref, p_ref = refs[2 * count + 1 :]
    cols = r_ref.shape[1]
    half = cols // 2
    for c in range(0, cols, half):
        total = base[r, :, pl.ds(c, half)]
        for e, b in zip(ext, w):
            total = total + dot(e[...], b[:, pl.ds(r * cols + c, half)])
        r_ref[:, pl.ds(c, half)] = total[:rows].astype(r_ref.dtype)
        p_ref[:, pl.ds(c, half)] = total[rows:].astype(p_ref.dtype)


def per_device(inputs, w_qkv, w_out, turn_ids, picked, owners, candidates):
    tokens_here, model_width = inputs.shape
    width = w_qkv.shape[2]
    heads_here = width // HDIM
    n_head = lax.axis_size("head")
    n_seq = lax.axis_size("seq")
    chips = n_head // 2
    half_bits = (chips.bit_length() - 1) // 2
    side = 1 << half_bits
    head = lax.axis_index("head")
    cols = model_width // n_head
    r_dev = picked.shape[1]
    steps = 8

    def along(m):
        return masks_of(half_bits, m)

    def across(r):
        return along(r)[::-1]

    def for_columns(w, m):
        return pl.pallas_call(
            functools.partial(cut_kernel, m=m, half_bits=half_bits),
            out_shape=jax.ShapeDtypeStruct((width, side * cols), BF16),
            in_specs=[ANY],
            out_specs=VMEM,
            scratch_shapes=[pltpu.SemaphoreType.DMA((side,))],
            cost_estimate=pl.CostEstimate(
                flops=0, bytes_accessed=4 * width * side * cols, transcendentals=0
            ),
            compiler_params=pltpu.CompilerParams(vmem_limit_bytes=4 << 20),
        )(w)

    w_in = [move(for_columns(stay(w_out), m), along(m)) for m in range(1, side)]
    w_peer = move(w_out, (1, 1))

    scratch = pltpu.VMEM
    keys, values, states, x_here = pl.pallas_call(
        functools.partial(kv_kernel, steps=steps),
        out_shape=[
            jax.ShapeDtypeStruct((tokens_here, width), BF16),
            jax.ShapeDtypeStruct((tokens_here, width), BF16),
            jax.ShapeDtypeStruct((heads_here, HDIM, HDIM), BF16),
            jax.ShapeDtypeStruct((tokens_here, model_width), BF16),
        ],
        in_specs=[HBM, HBM],
        out_specs=[VMEM] * 4,
        scratch_shapes=[
            scratch((2, model_width, width), BF16),
            scratch((2, tokens_here, width), F32),
            pltpu.SemaphoreType.DMA((3, steps)),
        ],
        cost_estimate=pl.CostEstimate(
            flops=4 * tokens_here * model_width * width,
            bytes_accessed=2 * model_width * (tokens_here + 2 * width),
            transcendentals=0,
        ),
        compiler_params=pltpu.CompilerParams(vmem_limit_bytes=24 << 20),
        name="kv",
    )(stay(inputs), stay(w_qkv))

    earlier = [
        lax.ppermute(states, "seq", [(i, i ^ s) for i in range(n_seq)]) for s in range(1, n_seq)
    ]

    w_in_peer = [move(for_columns(w_peer, m), along(m)) for m in range(1, side)]

    query, local = pl.pallas_call(
        functools.partial(q_kernel, steps=steps),
        out_shape=[
            jax.ShapeDtypeStruct((tokens_here, width), BF16),
            jax.ShapeDtypeStruct((tokens_here, width), F32),
        ],
        in_specs=[VMEM, HBM, VMEM, VMEM],
        out_specs=[VMEM] * 2,
        scratch_shapes=[
            scratch((model_width, width), BF16),
            scratch((tokens_here, width), F32),
            pltpu.SemaphoreType.DMA((steps,)),
        ],
        cost_estimate=pl.CostEstimate(
            flops=2 * tokens_here * model_width * width,
            bytes_accessed=2 * model_width * width,
            transcendentals=0,
        ),
        compiler_params=pltpu.CompilerParams(vmem_limit_bytes=10 << 20),
        name="qlocal",
    )(x_here, stay(w_qkv), keys, values)

    turn_row = turn_ids[0]
    pick_row = picked[0]
    tok_pos = jnp.arange(tokens_here, dtype=jnp.int32)
    pick_hot = tok_pos[None, :] == pick_row[:, None]
    sel_turn = jnp.sum(jnp.where(pick_hot, turn_row[None, :], 0), axis=1)
    member = (turn_row[None, :] == sel_turn[:, None]) & (tok_pos[None, :] <= pick_row[:, None])
    row_count = jnp.sum(member.astype(F32), axis=1)
    member = member.astype(BF16)

    ext = pl.pallas_call(
        functools.partial(attend_kernel, others=n_seq - 1),
        out_shape=jax.ShapeDtypeStruct((tokens_here + r_dev, width), BF16),
        in_specs=[VMEM] * (3 + n_seq - 1),
        out_specs=VMEM,
        compiler_params=pltpu.CompilerParams(vmem_limit_bytes=8 << 20),
        name="attend",
    )(query, local, member, *earlier)

    ext_peer = move(ext, (1, 1))
    ext_in = [move(ext, along(m)) for m in range(1, side)]
    ext_in_peer = [move(ext_peer, along(m)) for m in range(1, side)]

    height = tokens_here + r_dev
    base = pl.pallas_call(
        functools.partial(here_kernel, half_bits=half_bits),
        out_shape=jax.ShapeDtypeStruct((side, height, cols), F32),
        in_specs=[VMEM] * 3 + [HBM, HBM, ANY],
        out_specs=VMEM,
        scratch_shapes=[
            scratch((tokens_here, cols), BF16),
            scratch((side, 2, width, cols), BF16),
            pltpu.SemaphoreType.DMA((side + 1, 2)),
        ],
        cost_estimate=pl.CostEstimate(
            flops=4 * height * side * cols * width,
            bytes_accessed=4 * width * side * cols,
            transcendentals=0,
        ),
        compiler_params=pltpu.CompilerParams(vmem_limit_bytes=24 << 20),
        name="here",
    )(ext, ext_peer, member, stay(inputs), stay(w_out), w_peer)

    stacks = [*ext_in, *ext_in_peer]
    weights = [*w_in, *w_in_peer]

    def project(r, kind):
        return pl.pallas_call(
            functools.partial(add_kernel, count=len(stacks), r=r, rows=tokens_here),
            out_shape=[
                jax.ShapeDtypeStruct((tokens_here, cols), kind),
                jax.ShapeDtypeStruct((r_dev, cols), kind),
            ],
            in_specs=[VMEM] * (2 * len(stacks) + 1),
            out_specs=[VMEM] * 2,
            cost_estimate=pl.CostEstimate(
                flops=2 * height * cols * width * len(stacks),
                bytes_accessed=2 * width * cols * len(stacks),
                transcendentals=0,
            ),
            compiler_params=pltpu.CompilerParams(vmem_limit_bytes=12 << 20),
        )(*stacks, *weights, base)

    given = [project(r, BF16) for r in range(1, side)]
    pool_in = [move(p, across(r + 1)) for r, (_, p) in enumerate(given)]
    rows_in = [move(b, across(r + 1)) for r, (b, _) in enumerate(given)]
    rows_here, pooled = project(0, F32)

    for p in pool_in:
        pooled = pooled + p.astype(F32)
    summary = (pooled / row_count[:, None]).astype(BF16)
    summary_peer = move(summary, (1, 1))

    cap_rows = 4 * r_dev // n_head
    owner_row = owners[:, 0]
    row_pos = jnp.arange(r_dev, dtype=jnp.int32)
    head_pos = jnp.arange(n_head, dtype=jnp.int32)
    own_hot = (owner_row[:, None] == head_pos[None, :]).astype(jnp.int32)
    before = (row_pos[:, None] > row_pos[None, :]).astype(jnp.int32)
    slot_rank = jnp.sum(jnp.dot(before, own_hot) * own_hot, axis=1)
    slots = jnp.arange(cap_rows, dtype=jnp.int32)
    both = jnp.concatenate([summary, summary_peer], axis=1)
    scores = 0.0
    for j in range(chips):
        wanted = (owner_row == (head ^ (2 * j)))[None, :] & (slot_rank[None, :] == slots[:, None])
        rows = dot(wanted.astype(BF16), both).astype(BF16)
        if j:
            rows = move(rows, (2 * j, 2 * j))
        for c in range(2):
            cand = lax.dynamic_slice_in_dim(candidates, (head ^ (2 * j) ^ c) * cols, cols, 1)
            scores = scores + lax.dot_general(
                rows[:, c * cols : (c + 1) * cols],
                cand,
                (((1,), (1,)), ((), ())),
                preferred_element_type=F32,
            )

    total = rows_here
    for b in rows_in:
        total = total + b.astype(F32)
    return (total.astype(BF16), scores)


def solution(mesh):
    return jax.shard_map(
        per_device,
        mesh=mesh,
        in_specs=(
            P("seq", None),
            P(None, None, "head"),
            P("head", None),
            P("seq", None),
            P("seq", None),
            P("seq", None),
            P(("seq", "head"), None),
        ),
        out_specs=(P("seq", "head"), P(("seq", "head"), None)),
        check_vma=False,
    )
```

```python
import functools
import jax
import jax.numpy as jnp
from jax import lax
from jax.experimental import pallas as pl
from jax.experimental.pallas import tpu as pltpu
from jax.sharding import PartitionSpec as P


HDIM = 128
F32 = jnp.float32
BF16 = jnp.bfloat16
VMEM = pl.BlockSpec(memory_space=pltpu.VMEM)
HBM = pl.BlockSpec(memory_space=pltpu.HBM)


def move(value, masks):
    n = lax.axis_size("head")
    return lax.ppermute(value, "head", [(i, i ^ masks[i % 2]) for i in range(n)])


def dot(a, b):
    return jnp.dot(a, b, preferred_element_type=F32)


def masks_of(half_bits, m):
    return (m << 1, m << (1 + half_bits))


def place(half_bits, m, r, head=None):
    head = lax.axis_index("head") if head is None else head
    a, c = masks_of(half_bits, m), masks_of(half_bits, r)[::-1]
    return head ^ jnp.where(lax.bitwise_and(head, 1) == 0, a[0] ^ c[0], a[1] ^ c[1])


def block_of(index, size):
    return pl.ds(pl.multiple_of(index * size, size), size)


def kv_kernel(
    x_ref, w_ref, o_ref, k_ref, v_ref, s_ref, x_buf, cut_ref, w_buf, acc, sems, cut_sems, *, steps, half_bits
):
    depth = x_ref.shape[1] // steps
    copies = []
    for s in range(steps):
        at = pl.ds(s * depth, depth)
        copies.append(
            [pltpu.make_async_copy(x_ref.at[:, at], x_buf.at[:, at], sems.at[0, s])]
            + [
                pltpu.make_async_copy(w_ref.at[1 + i, at], w_buf.at[i, at], sems.at[1 + i, s])
                for i in range(2)
            ]
        )
        for copy in copies[-1]:
            copy.start()
    for_partner = cuts(o_ref, [cut_ref], cut_sems, [(True, 0)], half_bits)
    for copy in for_partner:
        copy.start()
    for s in range(steps):
        for copy in copies[s]:
            copy.wait()
        at = pl.ds(s * depth, depth)
        for i in range(2):
            part = dot(x_buf[:, at], w_buf[i, at])
            acc[i] = part if s == 0 else acc[i] + part
    k_ref[...] = acc[0].astype(BF16)
    v_ref[...] = acc[1].astype(BF16)
    for h in range(k_ref.shape[1] // HDIM):
        of = pl.ds(h * HDIM, HDIM)
        state = lax.dot_general(
            k_ref[:, of], v_ref[:, of], (((0,), (0,)), ((), ())), preferred_element_type=F32
        )
        s_ref[h] = state.astype(BF16)
    for copy in for_partner:
        copy.wait()


def q_kernel(x_ref, w_ref, k_ref, v_ref, q_ref, l_ref, w_buf, acc, sems, *, steps):
    depth = x_ref.shape[1] // steps
    copies = []
    for s in range(steps):
        at = pl.ds(s * depth, depth)
        copies.append(pltpu.make_async_copy(w_ref.at[0, at], w_buf.at[at], sems.at[s]))
        copies[-1].start()
    for s in range(steps):
        copies[s].wait()
        at = pl.ds(s * depth, depth)
        part = dot(x_ref[:, at], w_buf[at])
        acc[...] = part if s == 0 else acc[...] + part
    q_ref[...] = acc[...].astype(BF16)
    rows = q_ref.shape[0]
    block = min(rows, 256)
    for h in range(q_ref.shape[1] // HDIM):
        of = pl.ds(h * HDIM, HDIM)
        for b in range(0, rows, block):
            seen = b + block
            sc = lax.dot_general(
                q_ref[pl.ds(b, block), of],
                k_ref[pl.ds(0, seen), of],
                (((1,), (1,)), ((), ())),
                preferred_element_type=F32,
            )
            t = lax.broadcasted_iota(jnp.int32, sc.shape, 0) + b
            s = lax.broadcasted_iota(jnp.int32, sc.shape, 1)
            sc = jnp.where(t >= s, sc, 0.0).astype(BF16)
            l_ref[pl.ds(b, block), of] = dot(sc, v_ref[pl.ds(0, seen), of])


def attend_kernel(*refs, others):
    q_ref, l_ref, m_ref = refs[:3]
    states, out_ref = refs[3 : 3 + others], refs[3 + others]
    rows = q_ref.shape[0]
    seq = lax.axis_index("seq")
    for h in range(q_ref.shape[1] // HDIM):
        of = pl.ds(h * HDIM, HDIM)
        prefix = jnp.zeros((HDIM, HDIM), F32)
        for i, state in enumerate(states):
            prefix = prefix + jnp.where((seq ^ (i + 1)) < seq, state[h].astype(F32), 0.0)
        summed = l_ref[:, of] + dot(q_ref[:, of], prefix.astype(BF16))
        scale = lax.rsqrt(jnp.mean(summed * summed, axis=-1, keepdims=True) + 1e-05)
        attn = (summed * scale).astype(BF16)
        out_ref[pl.ds(0, rows), of] = attn
        out_ref[pl.ds(rows, m_ref.shape[0]), of] = dot(m_ref[...], attn).astype(BF16)


def stay(x):
    return pltpu.with_memory_space_constraint(x, pltpu.HBM)


def cuts(w_ref, outs, sems, jobs, half_bits):
    side = 1 << half_bits
    cols = outs[0].shape[1] // side
    head = lax.axis_index("head")
    copies = []
    for n, (partner, m) in enumerate(jobs):
        for r in range(side):
            at = place(half_bits, m, r, head ^ 1 if partner else head)
            copies.append(
                pltpu.make_async_copy(
                    w_ref.at[:, block_of(at, cols)],
                    outs[n].at[:, pl.ds(r * cols, cols)],
                    sems.at[n, r],
                )
            )
    return copies


def cut_kernel(w_ref, *refs, jobs, half_bits):
    copies = cuts(w_ref, refs[: len(jobs)], refs[-1], jobs, half_bits)
    for copy in copies:
        copy.start()
    for copy in copies:
        copy.wait()


def here_kernel(own_ref, peer_ref, m_ref, x_ref, w_ref, wp_ref, out_ref, x_buf, w_buf, sems, *, half_bits):
    side = 1 << half_bits
    cols = out_ref.shape[2]
    rows = m_ref.shape[1]
    order = list(range(1, side)) + [0]
    copies = {}
    for r in order:
        at = block_of(place(half_bits, 0, r), cols)
        copies[r] = pltpu.make_async_copy(w_ref.at[:, at], w_buf.at[r], sems.at[r])
        copies[r].start()
    own = pltpu.make_async_copy(
        x_ref.at[:, block_of(lax.axis_index("head"), cols)], x_buf, sems.at[side]
    )
    own.start()
    for r in order:
        part = dot(peer_ref[...], wp_ref[:, pl.ds(r * cols, cols)])
        copies[r].wait()
        out_ref[r] = part + dot(own_ref[...], w_buf[r])
    own.wait()
    out_ref[0, pl.ds(0, rows)] += x_buf[...].astype(F32)
    out_ref[0, pl.ds(rows, m_ref.shape[0])] += dot(m_ref[...], x_buf[...])


def add_kernel(*refs, count, r, rows):
    ext, w, base = refs[:count], refs[count : 2 * count], refs[2 * count]
    r_ref, p_ref, buf, sems = refs[2 * count + 1 :]
    cols = r_ref.shape[1]
    half = cols // 2
    copies = []
    for n, c in enumerate((0, half)):
        at = pl.ds(c, half)
        total = base[r, :, at]
        for e, b in zip(ext, w):
            total = total + dot(e[...], b[:, pl.ds(r * cols + c, half)])
        buf[:, at] = total[:rows].astype(buf.dtype)
        copies.append(pltpu.make_async_copy(buf.at[:, at], r_ref.at[:, at], sems.at[n]))
        copies[-1].start()
        p_ref[:, at] = total[rows:].astype(p_ref.dtype)
    for copy in copies:
        copy.wait()


def mix_kernel(*refs):
    parts, out_ref, buf, sems = refs[:-3], refs[-3], refs[-2], refs[-1]
    rows = buf.shape[0] // 4
    copies = []
    for n in range(4):
        at = pl.ds(n * rows, rows)
        total = parts[0][at]
        for part in parts[1:]:
            total = total + part[at].astype(F32)
        buf[at] = total.astype(BF16)
        copies.append(pltpu.make_async_copy(buf.at[at], out_ref.at[at], sems.at[n]))
        copies[-1].start()
    for copy in copies:
        copy.wait()


def score_kernel(*refs):
    c_ref, slots, out_ref = refs[0], refs[1:-1], refs[-1]
    cols = slots[0].shape[1] // 2
    head = lax.axis_index("head")
    total = jnp.zeros(out_ref.shape, F32)
    for j, rows in enumerate(slots):
        for c in range(2):
            total = total + lax.dot_general(
                rows[:, pl.ds(c * cols, cols)],
                c_ref[:, block_of(head ^ (2 * j + c), cols)],
                (((1,), (1,)), ((), ())),
                preferred_element_type=F32,
            )
    out_ref[...] = total


def per_device(inputs, w_qkv, w_out, turn_ids, picked, owners, candidates):
    tokens_here, model_width = inputs.shape
    width = w_qkv.shape[2]
    heads_here = width // HDIM
    n_head = lax.axis_size("head")
    n_seq = lax.axis_size("seq")
    chips = n_head // 2
    half_bits = (chips.bit_length() - 1) // 2
    side = 1 << half_bits
    head = lax.axis_index("head")
    cols = model_width // n_head
    r_dev = picked.shape[1]
    steps = 8

    def along(m):
        return masks_of(half_bits, m)

    def across(r):
        return along(r)[::-1]

    def beside(m):
        return tuple(mask ^ 1 for mask in across(m))

    jobs = [(partner, m) for partner in (False, True) for m in range(1, side)]
    cut = pl.pallas_call(
        functools.partial(cut_kernel, jobs=jobs, half_bits=half_bits),
        out_shape=[jax.ShapeDtypeStruct((width, side * cols), BF16)] * len(jobs),
        in_specs=[HBM],
        out_specs=[VMEM] * len(jobs),
        scratch_shapes=[pltpu.SemaphoreType.DMA((len(jobs), side))],
        cost_estimate=pl.CostEstimate(
            flops=0, bytes_accessed=4 * width * side * cols * len(jobs), transcendentals=0
        ),
        compiler_params=pltpu.CompilerParams(
            vmem_limit_bytes=2 * width * side * cols * len(jobs) + (1 << 20)
        ),
        name="cut",
    )(stay(w_out))
    w_in = [move(cut[m - 1], along(m)) for m in range(1, side)]
    w_in_peer = [move(cut[side + m - 2], beside(m)) for m in range(1, side)]

    scratch = pltpu.VMEM
    keys, values, states, x_here, w_own = pl.pallas_call(
        functools.partial(kv_kernel, steps=steps, half_bits=half_bits),
        out_shape=[
            jax.ShapeDtypeStruct((tokens_here, width), BF16),
            jax.ShapeDtypeStruct((tokens_here, width), BF16),
            jax.ShapeDtypeStruct((heads_here, HDIM, HDIM), BF16),
            jax.ShapeDtypeStruct((tokens_here, model_width), BF16),
            jax.ShapeDtypeStruct((width, side * cols), BF16),
        ],
        in_specs=[HBM] * 3,
        out_specs=[VMEM] * 5,
        scratch_shapes=[
            scratch((2, model_width, width), BF16),
            scratch((2, tokens_here, width), F32),
            pltpu.SemaphoreType.DMA((3, steps)),
            pltpu.SemaphoreType.DMA((1, side)),
        ],
        cost_estimate=pl.CostEstimate(
            flops=4 * tokens_here * model_width * width,
            bytes_accessed=2 * model_width * (tokens_here + 2 * width),
            transcendentals=0,
        ),
        compiler_params=pltpu.CompilerParams(vmem_limit_bytes=14 << 20),
        name="kv",
    )(stay(inputs), stay(w_qkv), stay(w_out))
    w_peer = move(w_own, (1, 1))

    earlier = [
        lax.ppermute(states, "seq", [(i, i ^ s) for i in range(n_seq)]) for s in range(1, n_seq)
    ]

    query, local = pl.pallas_call(
        functools.partial(q_kernel, steps=steps),
        out_shape=[
            jax.ShapeDtypeStruct((tokens_here, width), BF16),
            jax.ShapeDtypeStruct((tokens_here, width), F32),
        ],
        in_specs=[VMEM, HBM, VMEM, VMEM],
        out_specs=[VMEM] * 2,
        scratch_shapes=[
            scratch((model_width, width), BF16),
            scratch((tokens_here, width), F32),
            pltpu.SemaphoreType.DMA((steps,)),
        ],
        cost_estimate=pl.CostEstimate(
            flops=2 * tokens_here * model_width * width,
            bytes_accessed=2 * model_width * width,
            transcendentals=0,
        ),
        compiler_params=pltpu.CompilerParams(vmem_limit_bytes=10 << 20),
        name="qlocal",
    )(x_here, stay(w_qkv), keys, values)

    turn_row = turn_ids[0]
    pick_row = picked[0]
    tok_pos = jnp.arange(tokens_here, dtype=jnp.int32)
    pick_hot = tok_pos[None, :] == pick_row[:, None]
    sel_turn = jnp.sum(jnp.where(pick_hot, turn_row[None, :], 0), axis=1)
    member = (turn_row[None, :] == sel_turn[:, None]) & (tok_pos[None, :] <= pick_row[:, None])
    row_count = jnp.sum(member.astype(F32), axis=1)
    member = member.astype(BF16)

    ext = pl.pallas_call(
        functools.partial(attend_kernel, others=n_seq - 1),
        out_shape=jax.ShapeDtypeStruct((tokens_here + r_dev, width), BF16),
        in_specs=[VMEM] * (3 + n_seq - 1),
        out_specs=VMEM,
        compiler_params=pltpu.CompilerParams(vmem_limit_bytes=4 << 20),
        name="attend",
    )(query, local, member, *earlier)

    ext_in = [move(ext, along(m)) for m in range(1, side)]
    ext_in_peer = [move(ext, beside(m)) for m in range(1, side)]
    ext_peer = move(ext, (1, 1))

    height = tokens_here + r_dev
    base = pl.pallas_call(
        functools.partial(here_kernel, half_bits=half_bits),
        out_shape=jax.ShapeDtypeStruct((side, height, cols), F32),
        in_specs=[VMEM] * 3 + [HBM, HBM, VMEM],
        out_specs=VMEM,
        scratch_shapes=[
            scratch((tokens_here, cols), BF16),
            scratch((side, width, cols), BF16),
            pltpu.SemaphoreType.DMA((side + 1,)),
        ],
        cost_estimate=pl.CostEstimate(
            flops=4 * height * side * cols * width,
            bytes_accessed=4 * width * side * cols,
            transcendentals=0,
        ),
        compiler_params=pltpu.CompilerParams(vmem_limit_bytes=12 << 20),
        name="here",
    )(ext, ext_peer, member, stay(inputs), stay(w_out), w_peer)

    stacks = [*ext_in, *ext_in_peer]
    weights = [*w_in, *w_in_peer]

    def project(r, kind):
        return pl.pallas_call(
            functools.partial(add_kernel, count=len(stacks), r=r, rows=tokens_here),
            out_shape=[
                jax.ShapeDtypeStruct((tokens_here, cols), kind),
                jax.ShapeDtypeStruct((r_dev, cols), kind),
            ],
            in_specs=[VMEM] * (2 * len(stacks) + 1),
            out_specs=[HBM, VMEM],
            scratch_shapes=[
                scratch((tokens_here, cols), kind),
                pltpu.SemaphoreType.DMA((2,)),
            ],
            cost_estimate=pl.CostEstimate(
                flops=2 * height * cols * width * len(stacks),
                bytes_accessed=2 * width * cols * len(stacks),
                transcendentals=0,
            ),
            compiler_params=pltpu.CompilerParams(vmem_limit_bytes=12 << 20),
        )(*stacks, *weights, base)

    given = [project(r, BF16) for r in range(1, side)]
    pool_in = [move(p, across(r + 1)) for r, (_, p) in enumerate(given)]
    rows_in = [move(b, across(r + 1)) for r, (b, _) in enumerate(given)]
    rows_here, pooled = project(0, F32)

    for p in pool_in:
        pooled = pooled + p.astype(F32)
    summary = (pooled / row_count[:, None]).astype(BF16)
    summary_peer = move(summary, (1, 1))

    cap_rows = 4 * r_dev // n_head
    owner_row = owners[:, 0]
    row_pos = jnp.arange(r_dev, dtype=jnp.int32)
    head_pos = jnp.arange(n_head, dtype=jnp.int32)
    own_hot = (owner_row[:, None] == head_pos[None, :]).astype(jnp.int32)
    before = (row_pos[:, None] > row_pos[None, :]).astype(jnp.int32)
    slot_rank = jnp.sum(jnp.dot(before, own_hot) * own_hot, axis=1)
    slots = jnp.arange(cap_rows, dtype=jnp.int32)
    both = jnp.concatenate([summary, summary_peer], axis=1)
    found = []
    for j in range(chips):
        wanted = (owner_row == (head ^ (2 * j)))[None, :] & (slot_rank[None, :] == slots[:, None])
        rows = dot(wanted.astype(BF16), both).astype(BF16)
        found.append(move(rows, (2 * j, 2 * j)) if j else rows)

    mixed = pl.pallas_call(
        mix_kernel,
        out_shape=jax.ShapeDtypeStruct((tokens_here, cols), BF16),
        in_specs=[VMEM] * (1 + len(rows_in)),
        out_specs=HBM,
        scratch_shapes=[scratch((tokens_here, cols), BF16), pltpu.SemaphoreType.DMA((4,))],
        cost_estimate=pl.CostEstimate(
            flops=tokens_here * cols, bytes_accessed=8 * tokens_here * cols, transcendentals=0
        ),
        compiler_params=pltpu.CompilerParams(vmem_limit_bytes=4 << 20),
        name="mix",
    )(rows_here, *rows_in)
    scores = pl.pallas_call(
        score_kernel,
        out_shape=jax.ShapeDtypeStruct((cap_rows, candidates.shape[0]), F32),
        in_specs=[VMEM] * (1 + chips),
        out_specs=VMEM,
        compiler_params=pltpu.CompilerParams(vmem_limit_bytes=2 << 20),
        name="score",
    )(candidates, *found)
    return (mixed, scores)


def solution(mesh):
    return jax.shard_map(
        per_device,
        mesh=mesh,
        in_specs=(
            P("seq", None),
            P(None, None, "head"),
            P("head", None),
            P("seq", None),
            P("seq", None),
            P("seq", None),
            P(("seq", "head"), None),
        ),
        out_specs=(P("seq", "head"), P(("seq", "head"), None)),
        check_vma=False,
    )
```

```python
import functools
import jax
import jax.numpy as jnp
from jax import lax
from jax.experimental import pallas as pl
from jax.experimental.pallas import tpu as pltpu
from jax.sharding import PartitionSpec as P


HDIM = 128
F32 = jnp.float32
BF16 = jnp.bfloat16
VMEM = pl.BlockSpec(memory_space=pltpu.VMEM)
HBM = pl.BlockSpec(memory_space=pltpu.HBM)
ANY = pl.BlockSpec(memory_space=pl.ANY)


def move(value, masks):
    n = lax.axis_size("head")
    return lax.ppermute(value, "head", [(i, i ^ masks[i % 2]) for i in range(n)])


def dot(a, b):
    return jnp.dot(a, b, preferred_element_type=F32)


def masks_of(half_bits, m):
    return (m << 1, m << (1 + half_bits))


def place(half_bits, m, r, head=None):
    head = lax.axis_index("head") if head is None else head
    a, c = masks_of(half_bits, m), masks_of(half_bits, r)[::-1]
    return head ^ jnp.where(lax.bitwise_and(head, 1) == 0, a[0] ^ c[0], a[1] ^ c[1])


def block_of(index, size):
    return pl.ds(pl.multiple_of(index * size, size), size)


def kv_kernel(
    x_ref, w_ref, o_ref, k_ref, v_ref, s_ref, x_buf, own_ref, *refs, steps, half_bits
):
    side = 1 << half_bits
    mains, lates = refs[: side - 1], refs[side - 1 : 2 * side - 2]
    w_buf, acc, sems, cut_sems = refs[2 * side - 2 :]
    depth = x_ref.shape[1] // steps
    copies = []
    for s in range(steps):
        at = pl.ds(s * depth, depth)
        copies.append(
            [pltpu.make_async_copy(x_ref.at[:, at], x_buf.at[:, at], sems.at[0, s])]
            + [
                pltpu.make_async_copy(w_ref.at[1 + i, at], w_buf.at[i, at], sems.at[1 + i, s])
                for i in range(2)
            ]
        )
    cols = own_ref.shape[1] // side
    half = cols // 2
    partner = lax.bitwise_xor(lax.axis_index("head"), 1)
    cut = []

    def take(m, r, first, size, out, to):
        start = pl.multiple_of(place(half_bits, m, r, partner) * cols + first, half)
        cut.append(
            pltpu.make_async_copy(
                o_ref.at[:, pl.ds(start, size)], out.at[:, pl.ds(to, size)], cut_sems.at[len(cut)]
            )
        )

    for m in range(1, side):
        for r in range(1, side):
            take(m, r, 0, cols, mains[m - 1], (r - 1) * cols)
        take(m, 0, 0, half, mains[m - 1], (side - 1) * cols)
        take(m, 0, half, half, lates[m - 1], 0)
    for r in range(side):
        take(0, r, 0, cols, own_ref, r * cols)
    for copy in [*copies[0], *copies[1], *cut]:
        copy.start()
    for group in copies[2:]:
        for copy in group:
            copy.start()
    for s in range(steps):
        for copy in copies[s]:
            copy.wait()
        at = pl.ds(s * depth, depth)
        for i in range(2):
            part = dot(x_buf[:, at], w_buf[i, at])
            acc[i] = part if s == 0 else acc[i] + part
    k_ref[...] = acc[0].astype(BF16)
    v_ref[...] = acc[1].astype(BF16)
    for h in range(k_ref.shape[1] // HDIM):
        of = pl.ds(h * HDIM, HDIM)
        state = lax.dot_general(
            k_ref[:, of], v_ref[:, of], (((0,), (0,)), ((), ())), preferred_element_type=F32
        )
        s_ref[h] = state.astype(BF16)
    for copy in cut:
        copy.wait()


def q_kernel(x_ref, w_ref, k_ref, v_ref, q_ref, l_ref, w_buf, acc, sems, *, steps):
    depth = x_ref.shape[1] // steps
    rows = q_ref.shape[0]
    block = min(rows, 256)
    copies = []
    for s in range(steps):
        at = pl.ds(s * depth, depth)
        copies.append(pltpu.make_async_copy(w_ref.at[0, at], w_buf.at[at], sems.at[s]))
        copies[-1].start()
    for s in range(steps):
        copies[s].wait()
        at = pl.ds(s * depth, depth)
        for b in range(0, rows, block):
            part = dot(x_ref[pl.ds(b, block), at], w_buf[at])
            acc[pl.ds(b, block)] = part if s == 0 else acc[pl.ds(b, block)] + part
    q_ref[...] = acc[...].astype(BF16)
    for h in range(q_ref.shape[1] // HDIM):
        of = pl.ds(h * HDIM, HDIM)
        for b in range(0, rows, block):
            seen = b + block
            sc = lax.dot_general(
                q_ref[pl.ds(b, block), of],
                k_ref[pl.ds(0, seen), of],
                (((1,), (1,)), ((), ())),
                preferred_element_type=F32,
            )
            t = lax.broadcasted_iota(jnp.int32, sc.shape, 0) + b
            s = lax.broadcasted_iota(jnp.int32, sc.shape, 1)
            sc = jnp.where(t >= s, sc, 0.0).astype(BF16)
            l_ref[pl.ds(b, block), of] = dot(sc, v_ref[pl.ds(0, seen), of])


def attend_kernel(*refs, others):
    q_ref, l_ref, m_ref = refs[:3]
    states, out_ref = refs[3 : 3 + others], refs[3 + others]
    rows = q_ref.shape[0]
    seq = lax.axis_index("seq")
    for h in range(q_ref.shape[1] // HDIM):
        of = pl.ds(h * HDIM, HDIM)
        prefix = jnp.zeros((HDIM, HDIM), F32)
        for i, state in enumerate(states):
            prefix = prefix + jnp.where((seq ^ (i + 1)) < seq, state[h].astype(F32), 0.0)
        summed = l_ref[:, of] + dot(q_ref[:, of], prefix.astype(BF16))
        scale = lax.rsqrt(jnp.mean(summed * summed, axis=-1, keepdims=True) + 1e-05)
        attn = (summed * scale).astype(BF16)
        out_ref[pl.ds(0, rows), of] = attn
        out_ref[pl.ds(rows, m_ref.shape[0]), of] = dot(m_ref[...], attn).astype(BF16)


def stay(x):
    return pltpu.with_memory_space_constraint(x, pltpu.HBM)


def cut_kernel(w_ref, *refs, half_bits):
    outs, sems = refs[:-1], refs[-1]
    side = 1 << half_bits
    cols = outs[0].shape[1] // side
    copies = [
        pltpu.make_async_copy(
            w_ref.at[:, block_of(place(half_bits, m + 1, r), cols)],
            out.at[:, pl.ds(r * cols, cols)],
            sems.at[m, r],
        )
        for m, out in enumerate(outs)
        for r in range(side)
    ]
    for copy in copies:
        copy.start()
    for copy in copies:
        copy.wait()


def here_kernel(own_ref, peer_ref, m_ref, x_ref, w_ref, wp_ref, out_ref, e_buf, x_buf, w_buf, sems, *, half_bits):
    side = 1 << half_bits
    cols = out_ref.shape[2]
    rows, width = m_ref.shape[1], own_ref.shape[1]
    order = list(range(1, side)) + [0]
    copies = {}
    for r in order:
        at = block_of(place(half_bits, 0, r), cols)
        copies[r] = (
            pltpu.make_async_copy(w_ref.at[:, at], w_buf.at[r, pl.ds(0, width)], sems.at[r, 0]),
            pltpu.make_async_copy(
                wp_ref.at[:, pl.ds(r * cols, cols)], w_buf.at[r, pl.ds(width, width)], sems.at[r, 1]
            ),
        )
        for copy in copies[r]:
            copy.start()
    own = pltpu.make_async_copy(
        x_ref.at[:, block_of(lax.axis_index("head"), cols)], x_buf, sems.at[side, 0]
    )
    own.start()
    e_buf[:, pl.ds(0, width)] = own_ref[...]
    e_buf[:, pl.ds(width, width)] = peer_ref[...]
    block = e_buf.shape[0] // 2
    for r in order:
        for copy in copies[r]:
            copy.wait()
        for b in range(0, e_buf.shape[0], block):
            out_ref[r, pl.ds(b, block)] = dot(e_buf[pl.ds(b, block)], w_buf[r])
    own.wait()
    out_ref[0, pl.ds(0, rows)] += x_buf[...].astype(F32)
    out_ref[0, pl.ds(rows, m_ref.shape[0])] += dot(m_ref[...], x_buf[...])


def add_kernel(*refs, count, r, rows):
    ext, w = refs[: 2 * count], refs[2 * count : 4 * count]
    late, base = refs[4 * count : -5], refs[-5]
    r_ref, p_ref, buf, sems = refs[-4:]
    cols = r_ref.shape[1]
    half = cols // 2
    copies = []
    for n, c in enumerate((0, half)):
        at = pl.ds(c, half)
        total = base[r, :, at]
        for i in range(count):
            total = total + dot(ext[i][...], w[i][:, pl.ds(r * cols + c, half)])
            if r:
                part = w[count + i][:, pl.ds((r - 1) * cols + c, half)]
            elif n:
                part = late[i][...]
            else:
                part = w[count + i][:, pl.ds(w[count + i].shape[1] - half, half)]
            total = total + dot(ext[count + i][...], part)
        buf[:, at] = total[:rows].astype(buf.dtype)
        copies.append(pltpu.make_async_copy(buf.at[:, at], r_ref.at[:, at], sems.at[n]))
        copies[-1].start()
        p_ref[:, at] = total[rows:].astype(p_ref.dtype)
    for copy in copies:
        copy.wait()


def mix_kernel(*refs):
    parts, out_ref, buf, sems = refs[:-3], refs[-3], refs[-2], refs[-1]
    rows = buf.shape[0] // 4
    copies = []
    for n in range(4):
        at = pl.ds(n * rows, rows)
        total = parts[0][at]
        for part in parts[1:]:
            total = total + part[at].astype(F32)
        buf[at] = total.astype(BF16)
        copies.append(pltpu.make_async_copy(buf.at[at], out_ref.at[at], sems.at[n]))
        copies[-1].start()
    for copy in copies:
        copy.wait()


def score_kernel(*refs):
    c_ref, slots, out_ref = refs[0], refs[1:-1], refs[-1]
    cols = slots[0].shape[1] // 2
    head = lax.axis_index("head")
    total = jnp.zeros(out_ref.shape, F32)
    for j, rows in enumerate(slots):
        for c in range(2):
            total = total + lax.dot_general(
                rows[:, pl.ds(c * cols, cols)],
                c_ref[:, block_of(head ^ (2 * j + c), cols)],
                (((1,), (1,)), ((), ())),
                preferred_element_type=F32,
            )
    out_ref[...] = total


def per_device(inputs, w_qkv, w_out, turn_ids, picked, owners, candidates):
    tokens_here, model_width = inputs.shape
    width = w_qkv.shape[2]
    heads_here = width // HDIM
    n_head = lax.axis_size("head")
    n_seq = lax.axis_size("seq")
    chips = n_head // 2
    half_bits = (chips.bit_length() - 1) // 2
    side = 1 << half_bits
    head = lax.axis_index("head")
    cols = model_width // n_head
    r_dev = picked.shape[1]
    steps = 8

    def along(m):
        return masks_of(half_bits, m)

    def across(r):
        return along(r)[::-1]

    def beside(m):
        return tuple(mask ^ 1 for mask in across(m))

    cut = pl.pallas_call(
        functools.partial(cut_kernel, half_bits=half_bits),
        out_shape=[jax.ShapeDtypeStruct((width, side * cols), BF16)] * (side - 1),
        in_specs=[HBM],
        out_specs=[VMEM] * (side - 1),
        scratch_shapes=[pltpu.SemaphoreType.DMA((side - 1, side))],
        cost_estimate=pl.CostEstimate(
            flops=0, bytes_accessed=4 * width * side * cols * (side - 1), transcendentals=0
        ),
        compiler_params=pltpu.CompilerParams(
            vmem_limit_bytes=2 * width * side * cols * (side - 1) + (1 << 20)
        ),
        name="cut",
    )(stay(w_out))
    w_in = [move(c, along(m + 1)) for m, c in enumerate(cut)]

    scratch = pltpu.VMEM
    keys, values, states, x_here, w_own, *w_beside = pl.pallas_call(
        functools.partial(kv_kernel, steps=steps, half_bits=half_bits),
        out_shape=[
            jax.ShapeDtypeStruct((tokens_here, width), BF16),
            jax.ShapeDtypeStruct((tokens_here, width), BF16),
            jax.ShapeDtypeStruct((heads_here, HDIM, HDIM), BF16),
            jax.ShapeDtypeStruct((tokens_here, model_width), BF16),
            jax.ShapeDtypeStruct((width, side * cols), BF16),
            *[jax.ShapeDtypeStruct((width, side * cols - cols // 2), BF16)] * (side - 1),
            *[jax.ShapeDtypeStruct((width, cols // 2), BF16)] * (side - 1),
        ],
        in_specs=[HBM] * 3,
        out_specs=[VMEM] * (2 * side + 3),
        scratch_shapes=[
            scratch((2, model_width, width), BF16),
            scratch((2, tokens_here, width), F32),
            pltpu.SemaphoreType.DMA((3, steps)),
            pltpu.SemaphoreType.DMA(((side - 1) * (side + 1) + side,)),
        ],
        cost_estimate=pl.CostEstimate(
            flops=4 * tokens_here * model_width * width,
            bytes_accessed=2 * model_width * (tokens_here + 2 * width),
            transcendentals=0,
        ),
        compiler_params=pltpu.CompilerParams(vmem_limit_bytes=14 << 20),
        name="kv",
    )(stay(inputs), stay(w_qkv), stay(w_out))
    w_main = [move(w, beside(m + 1)) for m, w in enumerate(w_beside[: side - 1])]
    w_late = [move(w, beside(m + 1)) for m, w in enumerate(w_beside[side - 1 :])]
    w_peer = move(w_own, (1, 1))

    earlier = [
        lax.ppermute(states, "seq", [(i, i ^ s) for i in range(n_seq)]) for s in range(1, n_seq)
    ]

    query, local = pl.pallas_call(
        functools.partial(q_kernel, steps=4),
        out_shape=[
            jax.ShapeDtypeStruct((tokens_here, width), BF16),
            jax.ShapeDtypeStruct((tokens_here, width), F32),
        ],
        in_specs=[VMEM, HBM, VMEM, VMEM],
        out_specs=[VMEM] * 2,
        scratch_shapes=[
            scratch((model_width, width), BF16),
            scratch((tokens_here, width), F32),
            pltpu.SemaphoreType.DMA((4,)),
        ],
        cost_estimate=pl.CostEstimate(
            flops=2 * tokens_here * model_width * width,
            bytes_accessed=2 * model_width * width,
            transcendentals=0,
        ),
        compiler_params=pltpu.CompilerParams(vmem_limit_bytes=10 << 20),
        name="qlocal",
    )(x_here, stay(w_qkv), keys, values)

    turn_row = turn_ids[0]
    pick_row = picked[0]
    tok_pos = jnp.arange(tokens_here, dtype=jnp.int32)
    pick_hot = tok_pos[None, :] == pick_row[:, None]
    sel_turn = jnp.sum(jnp.where(pick_hot, turn_row[None, :], 0), axis=1)
    member = (turn_row[None, :] == sel_turn[:, None]) & (tok_pos[None, :] <= pick_row[:, None])
    row_count = jnp.sum(member.astype(F32), axis=1)
    member = member.astype(BF16)

    ext = pl.pallas_call(
        functools.partial(attend_kernel, others=n_seq - 1),
        out_shape=jax.ShapeDtypeStruct((tokens_here + r_dev, width), BF16),
        in_specs=[VMEM] * (3 + n_seq - 1),
        out_specs=VMEM,
        compiler_params=pltpu.CompilerParams(vmem_limit_bytes=4 << 20),
        name="attend",
    )(query, local, member, *earlier)

    ext_in = [move(ext, along(m)) for m in range(1, side)]
    ext_in_peer = [move(ext, beside(m)) for m in range(1, side)]
    ext_peer = move(ext, (1, 1))

    height = tokens_here + r_dev
    base = pl.pallas_call(
        functools.partial(here_kernel, half_bits=half_bits),
        out_shape=jax.ShapeDtypeStruct((side, height, cols), F32),
        in_specs=[VMEM] * 3 + [HBM, HBM, ANY],
        out_specs=VMEM,
        scratch_shapes=[
            scratch((height, 2 * width), BF16),
            scratch((tokens_here, cols), BF16),
            scratch((side, 2 * width, cols), BF16),
            pltpu.SemaphoreType.DMA((side + 1, 2)),
        ],
        cost_estimate=pl.CostEstimate(
            flops=4 * height * side * cols * width,
            bytes_accessed=4 * width * side * cols,
            transcendentals=0,
        ),
        compiler_params=pltpu.CompilerParams(vmem_limit_bytes=12 << 20),
        name="here",
    )(ext, ext_peer, member, stay(inputs), stay(w_out), w_peer)

    stacks = [*ext_in, *ext_in_peer]
    weights = [*w_in, *w_main]

    def project(r, kind):
        late = [] if r else w_late
        return pl.pallas_call(
            functools.partial(add_kernel, count=side - 1, r=r, rows=tokens_here),
            out_shape=[
                jax.ShapeDtypeStruct((tokens_here, cols), kind),
                jax.ShapeDtypeStruct((r_dev, cols), kind),
            ],
            in_specs=[VMEM] * (2 * len(stacks) + len(late) + 1),
            out_specs=[HBM, VMEM],
            scratch_shapes=[
                scratch((tokens_here, cols), kind),
                pltpu.SemaphoreType.DMA((2,)),
            ],
            cost_estimate=pl.CostEstimate(
                flops=2 * height * cols * width * len(stacks),
                bytes_accessed=2 * width * cols * len(stacks),
                transcendentals=0,
            ),
            compiler_params=pltpu.CompilerParams(vmem_limit_bytes=12 << 20),
        )(*stacks, *weights, *late, base)

    given = [project(r, BF16) for r in range(1, side)]
    pool_in = [move(p, across(r + 1)) for r, (_, p) in enumerate(given)]
    rows_in = [move(b, across(r + 1)) for r, (b, _) in enumerate(given)]
    rows_here, pooled = project(0, F32)

    for p in pool_in:
        pooled = pooled + p.astype(F32)
    summary = (pooled / row_count[:, None]).astype(BF16)
    summary_peer = move(summary, (1, 1))

    cap_rows = 4 * r_dev // n_head
    owner_row = owners[:, 0]
    row_pos = jnp.arange(r_dev, dtype=jnp.int32)
    head_pos = jnp.arange(n_head, dtype=jnp.int32)
    own_hot = (owner_row[:, None] == head_pos[None, :]).astype(jnp.int32)
    before = (row_pos[:, None] > row_pos[None, :]).astype(jnp.int32)
    slot_rank = jnp.sum(jnp.dot(before, own_hot) * own_hot, axis=1)
    slots = jnp.arange(cap_rows, dtype=jnp.int32)
    both = jnp.concatenate([summary, summary_peer], axis=1)
    found = []
    for j in range(chips):
        wanted = (owner_row == (head ^ (2 * j)))[None, :] & (slot_rank[None, :] == slots[:, None])
        rows = dot(wanted.astype(BF16), both).astype(BF16)
        found.append(move(rows, (2 * j, 2 * j)) if j else rows)

    mixed = pl.pallas_call(
        mix_kernel,
        out_shape=jax.ShapeDtypeStruct((tokens_here, cols), BF16),
        in_specs=[VMEM] * (1 + len(rows_in)),
        out_specs=HBM,
        scratch_shapes=[scratch((tokens_here, cols), BF16), pltpu.SemaphoreType.DMA((4,))],
        cost_estimate=pl.CostEstimate(
            flops=tokens_here * cols, bytes_accessed=8 * tokens_here * cols, transcendentals=0
        ),
        compiler_params=pltpu.CompilerParams(vmem_limit_bytes=4 << 20),
        name="mix",
    )(rows_here, *rows_in)
    scores = pl.pallas_call(
        score_kernel,
        out_shape=jax.ShapeDtypeStruct((cap_rows, candidates.shape[0]), F32),
        in_specs=[VMEM] * (1 + chips),
        out_specs=VMEM,
        compiler_params=pltpu.CompilerParams(vmem_limit_bytes=2 << 20),
        name="score",
    )(candidates, *found)
    return (mixed, scores)


def solution(mesh):
    return jax.shard_map(
        per_device,
        mesh=mesh,
        in_specs=(
            P("seq", None),
            P(None, None, "head"),
            P("head", None),
            P("seq", None),
            P("seq", None),
            P("seq", None),
            P(("seq", "head"), None),
        ),
        out_specs=(P("seq", "head"), P(("seq", "head"), None)),
        check_vma=False,
    )
```

```python
import functools
import jax
import jax.numpy as jnp
from jax import lax
from jax.experimental import pallas as pl
from jax.experimental.pallas import tpu as pltpu
from jax.sharding import PartitionSpec as P


HDIM = 128
F32 = jnp.float32
BF16 = jnp.bfloat16
VMEM = pl.BlockSpec(memory_space=pltpu.VMEM)
HBM = pl.BlockSpec(memory_space=pltpu.HBM)
ANY = pl.BlockSpec(memory_space=pl.ANY)


def move(value, masks):
    n = lax.axis_size("head")
    return lax.ppermute(value, "head", [(i, i ^ masks[i % 2]) for i in range(n)])


def dot(a, b):
    return jnp.dot(a, b, preferred_element_type=F32)


def masks_of(half_bits, m):
    return (m << 1, m << (1 + half_bits))


def place(half_bits, m, r, head=None):
    head = lax.axis_index("head") if head is None else head
    a, c = masks_of(half_bits, m), masks_of(half_bits, r)[::-1]
    return head ^ jnp.where(lax.bitwise_and(head, 1) == 0, a[0] ^ c[0], a[1] ^ c[1])


def block_of(index, size):
    return pl.ds(pl.multiple_of(index * size, size), size)


def cutter(w_ref, sems, cols, half_bits, partner):
    head = lax.axis_index("head")
    head = lax.bitwise_xor(head, 1) if partner else head
    copies = []

    def take(m, r, first, size, out, to):
        start = place(half_bits, m, r, head) * cols + first
        start = pl.multiple_of(start, cols // 2)
        copies.append(
            pltpu.make_async_copy(
                w_ref.at[:, pl.ds(start, size)], out.at[:, pl.ds(to, size)], sems.at[len(copies)]
            )
        )

    return copies, take


def kv_kernel(
    x_ref, w_ref, o_ref, k_ref, v_ref, s_ref, x_buf, *refs, steps, half_bits, cols
):
    side = 1 << half_bits
    mains = refs[: side - 1]
    w_buf, acc, sems, cut_sems = refs[side - 1 :]
    depth = x_ref.shape[1] // steps
    copies = []
    for s in range(steps):
        at = pl.ds(s * depth, depth)
        copies.append(
            [pltpu.make_async_copy(x_ref.at[:, at], x_buf.at[:, at], sems.at[0, s])]
            + [
                pltpu.make_async_copy(w_ref.at[1 + i, at], w_buf.at[i, at], sems.at[1 + i, s])
                for i in range(2)
            ]
        )
    cut, take = cutter(o_ref, cut_sems, cols, half_bits, True)
    for m in range(1, side):
        for r in range(1, side):
            take(m, r, 0, cols, mains[m - 1], (r - 1) * cols)
        take(m, 0, 0, cols // 2, mains[m - 1], (side - 1) * cols)
    for group in (*copies[:-2], cut, *copies[-2:]):
        for copy in group:
            copy.start()
    for s in range(steps):
        for copy in copies[s]:
            copy.wait()
        at = pl.ds(s * depth, depth)
        for i in range(2):
            part = dot(x_buf[:, at], w_buf[i, at])
            acc[i] = part if s == 0 else acc[i] + part
    k_ref[...] = acc[0].astype(BF16)
    v_ref[...] = acc[1].astype(BF16)
    for h in range(k_ref.shape[1] // HDIM):
        of = pl.ds(h * HDIM, HDIM)
        state = lax.dot_general(
            k_ref[:, of], v_ref[:, of], (((0,), (0,)), ((), ())), preferred_element_type=F32
        )
        s_ref[h] = state.astype(BF16)
    for copy in cut:
        copy.wait()


def q_kernel(
    x_ref, w_ref, k_ref, v_ref, o_ref, q_ref, l_ref, own_ref, *refs, steps, half_bits, cols
):
    side = 1 << half_bits
    lates = refs[: side - 1]
    w_buf, acc, sems, cut_sems = refs[side - 1 :]
    depth = x_ref.shape[1] // steps
    rows = q_ref.shape[0]
    block = min(rows, 256)
    copies = []
    for s in range(steps):
        at = pl.ds(s * depth, depth)
        copies.append(pltpu.make_async_copy(w_ref.at[0, at], w_buf.at[at], sems.at[s]))
        copies[-1].start()
    cut, take = cutter(o_ref, cut_sems, cols, half_bits, True)
    for r in range(side):
        take(0, r, 0, cols, own_ref, r * cols)
    for m in range(1, side):
        take(m, 0, cols // 2, cols // 2, lates[m - 1], 0)
    for copy in cut:
        copy.start()
    for s in range(steps):
        copies[s].wait()
        at = pl.ds(s * depth, depth)
        for b in range(0, rows, block):
            part = dot(x_ref[pl.ds(b, block), at], w_buf[at])
            acc[pl.ds(b, block)] = part if s == 0 else acc[pl.ds(b, block)] + part
    q_ref[...] = acc[...].astype(BF16)
    for h in range(q_ref.shape[1] // HDIM):
        of = pl.ds(h * HDIM, HDIM)
        for b in range(0, rows, block):
            seen = b + block
            sc = lax.dot_general(
                q_ref[pl.ds(b, block), of],
                k_ref[pl.ds(0, seen), of],
                (((1,), (1,)), ((), ())),
                preferred_element_type=F32,
            )
            t = lax.broadcasted_iota(jnp.int32, sc.shape, 0) + b
            s = lax.broadcasted_iota(jnp.int32, sc.shape, 1)
            sc = jnp.where(t >= s, sc, 0.0).astype(BF16)
            l_ref[pl.ds(b, block), of] = dot(sc, v_ref[pl.ds(0, seen), of])
    for copy in cut:
        copy.wait()


def attend_kernel(*refs, others):
    q_ref, l_ref = refs[:2]
    states, out_ref = refs[2 : 2 + others], refs[2 + others]
    seq = lax.axis_index("seq")
    for h in range(q_ref.shape[1] // HDIM):
        of = pl.ds(h * HDIM, HDIM)
        prefix = jnp.zeros((HDIM, HDIM), F32)
        for i, state in enumerate(states):
            prefix = prefix + jnp.where((seq ^ (i + 1)) < seq, state[h].astype(F32), 0.0)
        summed = l_ref[:, of] + dot(q_ref[:, of], prefix.astype(BF16))
        scale = lax.rsqrt(jnp.mean(summed * summed, axis=-1, keepdims=True) + 1e-05)
        out_ref[:, of] = (summed * scale).astype(BF16)


def stay(x):
    return pltpu.with_memory_space_constraint(x, pltpu.HBM)


def cut_kernel(w_ref, *refs, half_bits):
    outs, sems = refs[:-1], refs[-1]
    side = 1 << half_bits
    cols = outs[0].shape[1] // side
    copies = [
        pltpu.make_async_copy(
            w_ref.at[:, block_of(place(half_bits, m + 1, r), cols)],
            out.at[:, pl.ds(r * cols, cols)],
            sems.at[m, r],
        )
        for m, out in enumerate(outs)
        for r in range(side)
    ]
    for copy in copies:
        copy.start()
    for copy in copies:
        copy.wait()


def here_kernel(own_ref, peer_ref, m_ref, x_ref, w_ref, wp_ref, out_ref, e_buf, x_buf, w_buf, sems, *, half_bits):
    side = 1 << half_bits
    cols = out_ref.shape[2]
    rows, width = m_ref.shape[1], own_ref.shape[1]
    order = list(range(1, side)) + [0]
    copies = {}
    for r in order:
        at = block_of(place(half_bits, 0, r), cols)
        copies[r] = (
            pltpu.make_async_copy(w_ref.at[:, at], w_buf.at[r, pl.ds(0, width)], sems.at[r, 0]),
            pltpu.make_async_copy(
                wp_ref.at[:, pl.ds(r * cols, cols)], w_buf.at[r, pl.ds(width, width)], sems.at[r, 1]
            ),
        )
        for copy in copies[r]:
            copy.start()
    own = pltpu.make_async_copy(
        x_ref.at[:, block_of(lax.axis_index("head"), cols)], x_buf, sems.at[side, 0]
    )
    own.start()
    for i, ref in enumerate((own_ref, peer_ref)):
        at = pl.ds(i * width, width)
        e_buf[pl.ds(0, rows), at] = ref[...]
        e_buf[pl.ds(rows, m_ref.shape[0]), at] = dot(m_ref[...], ref[...]).astype(BF16)
    block = e_buf.shape[0] // 2
    for r in order:
        for copy in copies[r]:
            copy.wait()
        for b in range(0, e_buf.shape[0], block):
            out_ref[r, pl.ds(b, block)] = dot(e_buf[pl.ds(b, block)], w_buf[r])
    own.wait()
    out_ref[0, pl.ds(0, rows)] += x_buf[...].astype(F32)
    out_ref[0, pl.ds(rows, m_ref.shape[0])] += dot(m_ref[...], x_buf[...])


def add_kernel(*refs, count, r, rows):
    ext, w = refs[: 2 * count], refs[2 * count : 4 * count]
    late, m_ref, base = refs[4 * count : -6], refs[-6], refs[-5]
    r_ref, p_ref, buf, sems = refs[-4:]
    cols = r_ref.shape[1]
    half = cols // 2
    pooled = [dot(m_ref[...], e[...]).astype(BF16) for e in ext]
    copies = []
    for n, c in enumerate((0, half)):
        at = pl.ds(c, half)
        total, few = base[r, pl.ds(0, rows), at], base[r, pl.ds(rows, m_ref.shape[0]), at]
        for i in range(2 * count):
            if i < count:
                part = w[i][:, pl.ds(r * cols + c, half)]
            elif r:
                part = w[i][:, pl.ds((r - 1) * cols + c, half)]
            elif n:
                part = late[i - count][...]
            else:
                part = w[i][:, pl.ds(w[i].shape[1] - half, half)]
            total = total + dot(ext[i][...], part)
            few = few + dot(pooled[i], part)
        p_ref[:, at] = few.astype(p_ref.dtype)
        buf[:, at] = total.astype(buf.dtype)
        copies.append(pltpu.make_async_copy(buf.at[:, at], r_ref.at[:, at], sems.at[n]))
        copies[-1].start()
    for copy in copies:
        copy.wait()


def mix_kernel(*refs):
    parts, out_ref, buf, sems = refs[:-3], refs[-3], refs[-2], refs[-1]
    rows = buf.shape[0] // 4
    copies = []
    for n in range(4):
        at = pl.ds(n * rows, rows)
        total = parts[0][at]
        for part in parts[1:]:
            total = total + part[at].astype(F32)
        buf[at] = total.astype(BF16)
        copies.append(pltpu.make_async_copy(buf.at[at], out_ref.at[at], sems.at[n]))
        copies[-1].start()
    for copy in copies:
        copy.wait()


def score_kernel(c_ref, *refs, steps, add):
    slots, out_ref = refs[: len(steps)], refs[-1]
    cols = slots[0].shape[1] // 2
    head = lax.axis_index("head")
    total = refs[-2][...] if add else jnp.zeros(out_ref.shape, F32)
    for j, rows in zip(steps, slots):
        for c in range(2):
            total = total + lax.dot_general(
                rows[:, pl.ds(c * cols, cols)],
                c_ref[:, block_of(head ^ (2 * j + c), cols)],
                (((1,), (1,)), ((), ())),
                preferred_element_type=F32,
            )
    out_ref[...] = total


def per_device(inputs, w_qkv, w_out, turn_ids, picked, owners, candidates):
    tokens_here, model_width = inputs.shape
    width = w_qkv.shape[2]
    heads_here = width // HDIM
    n_head = lax.axis_size("head")
    n_seq = lax.axis_size("seq")
    chips = n_head // 2
    half_bits = (chips.bit_length() - 1) // 2
    side = 1 << half_bits
    head = lax.axis_index("head")
    cols = model_width // n_head
    r_dev = picked.shape[1]
    steps = 8

    def along(m):
        return masks_of(half_bits, m)

    def across(r):
        return along(r)[::-1]

    def beside(m):
        return tuple(mask ^ 1 for mask in across(m))

    cut = pl.pallas_call(
        functools.partial(cut_kernel, half_bits=half_bits),
        out_shape=[jax.ShapeDtypeStruct((width, side * cols), BF16)] * (side - 1),
        in_specs=[HBM],
        out_specs=[VMEM] * (side - 1),
        scratch_shapes=[pltpu.SemaphoreType.DMA((side - 1, side))],
        cost_estimate=pl.CostEstimate(
            flops=0, bytes_accessed=4 * width * side * cols * (side - 1), transcendentals=0
        ),
        compiler_params=pltpu.CompilerParams(
            vmem_limit_bytes=2 * width * side * cols * (side - 1) + (1 << 20)
        ),
        name="cut",
    )(stay(w_out))
    w_in = [move(c, along(m + 1)) for m, c in enumerate(cut)]

    scratch = pltpu.VMEM
    keys, values, states, x_here, *w_beside = pl.pallas_call(
        functools.partial(kv_kernel, steps=steps, half_bits=half_bits, cols=cols),
        out_shape=[
            jax.ShapeDtypeStruct((tokens_here, width), BF16),
            jax.ShapeDtypeStruct((tokens_here, width), BF16),
            jax.ShapeDtypeStruct((heads_here, HDIM, HDIM), BF16),
            jax.ShapeDtypeStruct((tokens_here, model_width), BF16),
            *[jax.ShapeDtypeStruct((width, side * cols - cols // 2), BF16)] * (side - 1),
        ],
        in_specs=[HBM] * 3,
        out_specs=[VMEM] * (side + 3),
        scratch_shapes=[
            scratch((2, model_width, width), BF16),
            scratch((2, tokens_here, width), F32),
            pltpu.SemaphoreType.DMA((3, steps)),
            pltpu.SemaphoreType.DMA(((side - 1) * side,)),
        ],
        cost_estimate=pl.CostEstimate(
            flops=4 * tokens_here * model_width * width,
            bytes_accessed=2 * model_width * (tokens_here + 2 * width),
            transcendentals=0,
        ),
        compiler_params=pltpu.CompilerParams(vmem_limit_bytes=14 << 20),
        name="kv",
    )(stay(inputs), stay(w_qkv), stay(w_out))
    w_main = [move(w, beside(m + 1)) for m, w in enumerate(w_beside)]

    earlier = [
        lax.ppermute(states, "seq", [(i, i ^ s) for i in range(n_seq)]) for s in range(1, n_seq)
    ]

    query, local, w_own, *w_rest = pl.pallas_call(
        functools.partial(q_kernel, steps=4, half_bits=half_bits, cols=cols),
        out_shape=[
            jax.ShapeDtypeStruct((tokens_here, width), BF16),
            jax.ShapeDtypeStruct((tokens_here, width), F32),
            jax.ShapeDtypeStruct((width, side * cols), BF16),
            *[jax.ShapeDtypeStruct((width, cols // 2), BF16)] * (side - 1),
        ],
        in_specs=[VMEM, HBM, VMEM, VMEM, HBM],
        out_specs=[VMEM] * (side + 2),
        scratch_shapes=[
            scratch((model_width, width), BF16),
            scratch((tokens_here, width), F32),
            pltpu.SemaphoreType.DMA((4,)),
            pltpu.SemaphoreType.DMA((2 * side - 1,)),
        ],
        cost_estimate=pl.CostEstimate(
            flops=2 * tokens_here * model_width * width,
            bytes_accessed=2 * model_width * width,
            transcendentals=0,
        ),
        compiler_params=pltpu.CompilerParams(vmem_limit_bytes=10 << 20),
        name="qlocal",
    )(x_here, stay(w_qkv), keys, values, stay(w_out))
    w_late = [move(w, beside(m + 1)) for m, w in enumerate(w_rest)]
    w_peer = move(w_own, (1, 1))

    turn_row = turn_ids[0]
    pick_row = picked[0]
    tok_pos = jnp.arange(tokens_here, dtype=jnp.int32)
    pick_hot = tok_pos[None, :] == pick_row[:, None]
    sel_turn = jnp.sum(jnp.where(pick_hot, turn_row[None, :], 0), axis=1)
    member = (turn_row[None, :] == sel_turn[:, None]) & (tok_pos[None, :] <= pick_row[:, None])
    row_count = jnp.sum(member.astype(F32), axis=1)
    member = member.astype(BF16)

    ext = pl.pallas_call(
        functools.partial(attend_kernel, others=n_seq - 1),
        out_shape=jax.ShapeDtypeStruct((tokens_here, width), BF16),
        in_specs=[VMEM] * (2 + n_seq - 1),
        out_specs=VMEM,
        compiler_params=pltpu.CompilerParams(vmem_limit_bytes=4 << 20),
        name="attend",
    )(query, local, *earlier)

    ext_in = [move(ext, along(m)) for m in range(1, side)]
    ext_in_peer = [move(ext, beside(m)) for m in range(1, side)]
    ext_peer = move(ext, (1, 1))

    height = tokens_here + r_dev
    base = pl.pallas_call(
        functools.partial(here_kernel, half_bits=half_bits),
        out_shape=jax.ShapeDtypeStruct((side, height, cols), F32),
        in_specs=[VMEM] * 3 + [HBM, HBM, ANY],
        out_specs=VMEM,
        scratch_shapes=[
            scratch((height, 2 * width), BF16),
            scratch((tokens_here, cols), BF16),
            scratch((side, 2 * width, cols), BF16),
            pltpu.SemaphoreType.DMA((side + 1, 2)),
        ],
        cost_estimate=pl.CostEstimate(
            flops=4 * height * side * cols * width,
            bytes_accessed=4 * width * side * cols,
            transcendentals=0,
        ),
        compiler_params=pltpu.CompilerParams(vmem_limit_bytes=12 << 20),
        name="here",
    )(ext, ext_peer, member, stay(inputs), stay(w_out), w_peer)

    stacks = [*ext_in, *ext_in_peer]
    weights = [*w_in, *w_main]

    def project(r, kind):
        late = [] if r else w_late
        return pl.pallas_call(
            functools.partial(add_kernel, count=side - 1, r=r, rows=tokens_here),
            out_shape=[
                jax.ShapeDtypeStruct((tokens_here, cols), kind),
                jax.ShapeDtypeStruct((r_dev, cols), kind),
            ],
            in_specs=[VMEM] * (2 * len(stacks) + len(late) + 2),
            out_specs=[HBM, VMEM],
            scratch_shapes=[
                scratch((tokens_here, cols), kind),
                pltpu.SemaphoreType.DMA((2,)),
            ],
            cost_estimate=pl.CostEstimate(
                flops=2 * height * cols * width * len(stacks),
                bytes_accessed=2 * width * cols * len(stacks),
                transcendentals=0,
            ),
            compiler_params=pltpu.CompilerParams(vmem_limit_bytes=12 << 20),
        )(*stacks, *weights, *late, member, base)

    given = [project(r, BF16) for r in range(1, side)]
    pool_in = [move(p, across(r + 1)) for r, (_, p) in enumerate(given)]
    rows_in = [move(b, across(r + 1)) for r, (b, _) in enumerate(given)]
    rows_here, pooled = project(0, F32)

    for p in pool_in:
        pooled = pooled + p.astype(F32)
    summary = (pooled / row_count[:, None]).astype(BF16)
    summary_peer = move(summary, (1, 1))

    cap_rows = 4 * r_dev // n_head
    owner_row = owners[:, 0]
    row_pos = jnp.arange(r_dev, dtype=jnp.int32)
    head_pos = jnp.arange(n_head, dtype=jnp.int32)
    own_hot = (owner_row[:, None] == head_pos[None, :]).astype(jnp.int32)
    before = (row_pos[:, None] > row_pos[None, :]).astype(jnp.int32)
    slot_rank = jnp.sum(jnp.dot(before, own_hot) * own_hot, axis=1)
    slots = jnp.arange(cap_rows, dtype=jnp.int32)
    both = jnp.concatenate([summary, summary_peer], axis=1)
    found = []
    for j in range(chips):
        wanted = (owner_row == (head ^ (2 * j)))[None, :] & (slot_rank[None, :] == slots[:, None])
        rows = dot(wanted.astype(BF16), both).astype(BF16)
        found.append(move(rows, (2 * j, 2 * j)) if j else rows)

    mixed = pl.pallas_call(
        mix_kernel,
        out_shape=jax.ShapeDtypeStruct((tokens_here, cols), BF16),
        in_specs=[VMEM] * (1 + len(rows_in)),
        out_specs=HBM,
        scratch_shapes=[scratch((tokens_here, cols), BF16), pltpu.SemaphoreType.DMA((4,))],
        cost_estimate=pl.CostEstimate(
            flops=tokens_here * cols, bytes_accessed=8 * tokens_here * cols, transcendentals=0
        ),
        compiler_params=pltpu.CompilerParams(vmem_limit_bytes=4 << 20),
        name="mix",
    )(rows_here, *rows_in)

    def score(steps, *before):
        return pl.pallas_call(
            functools.partial(score_kernel, steps=steps, add=bool(before)),
            out_shape=jax.ShapeDtypeStruct((cap_rows, candidates.shape[0]), F32),
            in_specs=[VMEM] * (1 + len(steps) + len(before)),
            out_specs=VMEM,
            compiler_params=pltpu.CompilerParams(vmem_limit_bytes=2 << 20),
            name="score" if before else "score_first",
        )(candidates, *[found[j] for j in steps], *before)

    scores = score(range(1, chips), score(range(1)))
    return (mixed, scores)


def solution(mesh):
    return jax.shard_map(
        per_device,
        mesh=mesh,
        in_specs=(
            P("seq", None),
            P(None, None, "head"),
            P("head", None),
            P("seq", None),
            P("seq", None),
            P("seq", None),
            P(("seq", "head"), None),
        ),
        out_specs=(P("seq", "head"), P(("seq", "head"), None)),
        check_vma=False,
    )
```

```python
import functools
import jax
import jax.numpy as jnp
from jax import lax
from jax.experimental import pallas as pl
from jax.experimental.pallas import tpu as pltpu
from jax.sharding import PartitionSpec as P


HDIM = 128
F32 = jnp.float32
BF16 = jnp.bfloat16
VMEM = pl.BlockSpec(memory_space=pltpu.VMEM)
HBM = pl.BlockSpec(memory_space=pltpu.HBM)
ANY = pl.BlockSpec(memory_space=pl.ANY)


def move(value, masks):
    n = lax.axis_size("head")
    return lax.ppermute(value, "head", [(i, i ^ masks[i % 2]) for i in range(n)])


def dot(a, b):
    return jnp.dot(a, b, preferred_element_type=F32)


def masks_of(half_bits, m):
    return (m << 1, m << (1 + half_bits))


def place(half_bits, m, r, head=None):
    head = lax.axis_index("head") if head is None else head
    a, c = masks_of(half_bits, m), masks_of(half_bits, r)[::-1]
    return head ^ jnp.where(lax.bitwise_and(head, 1) == 0, a[0] ^ c[0], a[1] ^ c[1])


def block_of(index, size):
    return pl.ds(pl.multiple_of(index * size, size), size)


def early_of(cols):
    return max(HDIM, cols // 4)


def cutter(w_ref, sems, cols, half_bits, partner):
    head = lax.axis_index("head")
    head = lax.bitwise_xor(head, 1) if partner else head
    copies = []

    def take(m, r, first, size, out, to):
        start = place(half_bits, m, r, head) * cols + first
        start = pl.multiple_of(start, early_of(cols))
        copies.append(
            pltpu.make_async_copy(
                w_ref.at[:, pl.ds(start, size)], out.at[:, pl.ds(to, size)], sems.at[len(copies)]
            )
        )

    return copies, take


def kv_kernel(
    x_ref, w_ref, o_ref, k_ref, v_ref, s_ref, x_buf, *refs, steps, half_bits, cols
):
    side = 1 << half_bits
    mains = refs[: side - 1]
    w_buf, acc, sems, cut_sems = refs[side - 1 :]
    depth = x_ref.shape[1] // steps
    copies = []
    for s in range(steps):
        at = pl.ds(s * depth, depth)
        copies.append(
            [pltpu.make_async_copy(x_ref.at[:, at], x_buf.at[:, at], sems.at[0, s])]
            + [
                pltpu.make_async_copy(w_ref.at[1 + i, at], w_buf.at[i, at], sems.at[1 + i, s])
                for i in range(2)
            ]
        )
    cut, take = cutter(o_ref, cut_sems, cols, half_bits, True)
    for m in range(1, side):
        for r in range(1, side):
            take(m, r, 0, cols, mains[m - 1], (r - 1) * cols)
        take(m, 0, 0, early_of(cols), mains[m - 1], (side - 1) * cols)
    for group in (*copies[:-2], cut, *copies[-2:]):
        for copy in group:
            copy.start()
    for s in range(steps):
        for copy in copies[s]:
            copy.wait()
        at = pl.ds(s * depth, depth)
        for i in range(2):
            part = dot(x_buf[:, at], w_buf[i, at])
            acc[i] = part if s == 0 else acc[i] + part
    k_ref[...] = acc[0].astype(BF16)
    v_ref[...] = acc[1].astype(BF16)
    for h in range(k_ref.shape[1] // HDIM):
        of = pl.ds(h * HDIM, HDIM)
        state = lax.dot_general(
            k_ref[:, of], v_ref[:, of], (((0,), (0,)), ((), ())), preferred_element_type=F32
        )
        s_ref[h] = state.astype(BF16)
    for copy in cut:
        copy.wait()


def q_kernel(
    x_ref, w_ref, k_ref, v_ref, o_ref, q_ref, l_ref, own_ref, *refs, steps, half_bits, cols
):
    side = 1 << half_bits
    lates = refs[: side - 1]
    w_buf, acc, sems, cut_sems = refs[side - 1 :]
    depth = x_ref.shape[1] // steps
    rows = q_ref.shape[0]
    block = min(rows, 256)
    copies = []
    for s in range(steps):
        at = pl.ds(s * depth, depth)
        copies.append(pltpu.make_async_copy(w_ref.at[0, at], w_buf.at[at], sems.at[s]))
        copies[-1].start()
    cut, take = cutter(o_ref, cut_sems, cols, half_bits, True)
    for r in range(side):
        take(0, r, 0, cols, own_ref, r * cols)
    for m in range(1, side):
        take(m, 0, early_of(cols), cols - early_of(cols), lates[m - 1], 0)
    for copy in cut:
        copy.start()
    for s in range(steps):
        copies[s].wait()
        at = pl.ds(s * depth, depth)
        for b in range(0, rows, block):
            part = dot(x_ref[pl.ds(b, block), at], w_buf[at])
            acc[pl.ds(b, block)] = part if s == 0 else acc[pl.ds(b, block)] + part
    q_ref[...] = acc[...].astype(BF16)
    for h in range(q_ref.shape[1] // HDIM):
        of = pl.ds(h * HDIM, HDIM)
        for b in range(0, rows, block):
            seen = b + block
            sc = lax.dot_general(
                q_ref[pl.ds(b, block), of],
                k_ref[pl.ds(0, seen), of],
                (((1,), (1,)), ((), ())),
                preferred_element_type=F32,
            )
            t = lax.broadcasted_iota(jnp.int32, sc.shape, 0) + b
            s = lax.broadcasted_iota(jnp.int32, sc.shape, 1)
            sc = jnp.where(t >= s, sc, 0.0).astype(BF16)
            l_ref[pl.ds(b, block), of] = dot(sc, v_ref[pl.ds(0, seen), of])
    for copy in cut:
        copy.wait()


def attend_kernel(*refs, others):
    q_ref, l_ref = refs[:2]
    states, out_ref = refs[2 : 2 + others], refs[2 + others]
    seq = lax.axis_index("seq")
    for h in range(q_ref.shape[1] // HDIM):
        of = pl.ds(h * HDIM, HDIM)
        prefix = jnp.zeros((HDIM, HDIM), F32)
        for i, state in enumerate(states):
            prefix = prefix + jnp.where((seq ^ (i + 1)) < seq, state[h].astype(F32), 0.0)
        summed = l_ref[:, of] + dot(q_ref[:, of], prefix.astype(BF16))
        scale = lax.rsqrt(jnp.mean(summed * summed, axis=-1, keepdims=True) + 1e-05)
        out_ref[:, of] = (summed * scale).astype(BF16)


def stay(x):
    return pltpu.with_memory_space_constraint(x, pltpu.HBM)


def cut_kernel(w_ref, *refs, half_bits):
    outs, sems = refs[:-1], refs[-1]
    side = 1 << half_bits
    cols = outs[0].shape[1] // side
    copies = [
        pltpu.make_async_copy(
            w_ref.at[:, block_of(place(half_bits, m + 1, r), cols)],
            out.at[:, pl.ds(r * cols, cols)],
            sems.at[m, r],
        )
        for m, out in enumerate(outs)
        for r in range(side)
    ]
    for copy in copies:
        copy.start()
    for copy in copies:
        copy.wait()


def here_kernel(own_ref, peer_ref, m_ref, x_ref, w_ref, wp_ref, out_ref, e_buf, x_buf, w_buf, sems, *, half_bits):
    side = 1 << half_bits
    cols = out_ref.shape[2]
    rows, width = m_ref.shape[1], own_ref.shape[1]
    order = list(range(1, side)) + [0]
    copies = {}
    for r in order:
        at = block_of(place(half_bits, 0, r), cols)
        copies[r] = (
            pltpu.make_async_copy(w_ref.at[:, at], w_buf.at[r, pl.ds(0, width)], sems.at[r, 0]),
            pltpu.make_async_copy(
                wp_ref.at[:, pl.ds(r * cols, cols)], w_buf.at[r, pl.ds(width, width)], sems.at[r, 1]
            ),
        )
        for copy in copies[r]:
            copy.start()
    own = pltpu.make_async_copy(
        x_ref.at[:, block_of(lax.axis_index("head"), cols)], x_buf, sems.at[side, 0]
    )
    own.start()
    for i, ref in enumerate((own_ref, peer_ref)):
        at = pl.ds(i * width, width)
        e_buf[pl.ds(0, rows), at] = ref[...]
        e_buf[pl.ds(rows, m_ref.shape[0]), at] = dot(m_ref[...], ref[...]).astype(BF16)
    block = e_buf.shape[0] // 2
    for r in order:
        for copy in copies[r]:
            copy.wait()
        for b in range(0, e_buf.shape[0], block):
            out_ref[r, pl.ds(b, block)] = dot(e_buf[pl.ds(b, block)], w_buf[r])
    own.wait()
    out_ref[0, pl.ds(0, rows)] += x_buf[...].astype(F32)
    out_ref[0, pl.ds(rows, m_ref.shape[0])] += dot(m_ref[...], x_buf[...])


def add_kernel(*refs, count, r, rows):
    ext, w = refs[: 2 * count], refs[2 * count : 4 * count]
    late, m_ref, base = refs[4 * count : -4], refs[-4], refs[-3]
    r_ref, p_ref = refs[-2:]
    cols = r_ref.shape[1]
    pooled = [dot(m_ref[...], e[...]).astype(BF16) for e in ext]
    split = cols // 2 if r else early_of(cols)
    for first, size in ((0, split), (split, cols - split)):
        at = pl.ds(first, size)
        total, few = base[r, pl.ds(0, rows), at], base[r, pl.ds(rows, m_ref.shape[0]), at]
        for i in range(2 * count):
            if i < count:
                part = w[i][:, pl.ds(r * cols + first, size)]
            elif r:
                part = w[i][:, pl.ds((r - 1) * cols + first, size)]
            elif first:
                part = late[i - count][...]
            else:
                part = w[i][:, pl.ds(w[i].shape[1] - size, size)]
            total = total + dot(ext[i][...], part)
            few = few + dot(pooled[i], part)
        p_ref[:, at] = few.astype(p_ref.dtype)
        r_ref[:, at] = total.astype(r_ref.dtype)


def mix_kernel(*refs):
    parts, out_ref, buf, sems = refs[:-3], refs[-3], refs[-2], refs[-1]
    rows = buf.shape[0] // 4
    copies = []
    for n in range(4):
        at = pl.ds(n * rows, rows)
        total = parts[0][at]
        for part in parts[1:]:
            total = total + part[at].astype(F32)
        buf[at] = total.astype(BF16)
        copies.append(pltpu.make_async_copy(buf.at[at], out_ref.at[at], sems.at[n]))
        copies[-1].start()
    for copy in copies:
        copy.wait()


def score_kernel(c_ref, *refs, steps, add):
    slots, out_ref = refs[: len(steps)], refs[-1]
    cols = slots[0].shape[1] // 2
    head = lax.axis_index("head")
    total = refs[-2][...] if add else jnp.zeros(out_ref.shape, F32)
    for j, rows in zip(steps, slots):
        for c in range(2):
            total = total + lax.dot_general(
                rows[:, pl.ds(c * cols, cols)],
                c_ref[:, block_of(head ^ (2 * j + c), cols)],
                (((1,), (1,)), ((), ())),
                preferred_element_type=F32,
            )
    out_ref[...] = total


def per_device(inputs, w_qkv, w_out, turn_ids, picked, owners, candidates):
    tokens_here, model_width = inputs.shape
    width = w_qkv.shape[2]
    heads_here = width // HDIM
    n_head = lax.axis_size("head")
    n_seq = lax.axis_size("seq")
    chips = n_head // 2
    half_bits = (chips.bit_length() - 1) // 2
    side = 1 << half_bits
    head = lax.axis_index("head")
    cols = model_width // n_head
    r_dev = picked.shape[1]
    steps = 8

    def along(m):
        return masks_of(half_bits, m)

    def across(r):
        return along(r)[::-1]

    def beside(m):
        return tuple(mask ^ 1 for mask in across(m))

    cut = pl.pallas_call(
        functools.partial(cut_kernel, half_bits=half_bits),
        out_shape=[jax.ShapeDtypeStruct((width, side * cols), BF16)] * (side - 1),
        in_specs=[HBM],
        out_specs=[VMEM] * (side - 1),
        scratch_shapes=[pltpu.SemaphoreType.DMA((side - 1, side))],
        cost_estimate=pl.CostEstimate(
            flops=0, bytes_accessed=4 * width * side * cols * (side - 1), transcendentals=0
        ),
        compiler_params=pltpu.CompilerParams(
            vmem_limit_bytes=2 * width * side * cols * (side - 1) + (1 << 20)
        ),
        name="cut",
    )(stay(w_out))
    w_in = [move(c, along(m + 1)) for m, c in enumerate(cut)]

    scratch = pltpu.VMEM
    keys, values, states, x_here, *w_beside = pl.pallas_call(
        functools.partial(kv_kernel, steps=steps, half_bits=half_bits, cols=cols),
        out_shape=[
            jax.ShapeDtypeStruct((tokens_here, width), BF16),
            jax.ShapeDtypeStruct((tokens_here, width), BF16),
            jax.ShapeDtypeStruct((heads_here, HDIM, HDIM), BF16),
            jax.ShapeDtypeStruct((tokens_here, model_width), BF16),
            *[jax.ShapeDtypeStruct((width, (side - 1) * cols + early_of(cols)), BF16)] * (side - 1),
        ],
        in_specs=[HBM] * 3,
        out_specs=[VMEM] * (side + 3),
        scratch_shapes=[
            scratch((2, model_width, width), BF16),
            scratch((2, tokens_here, width), F32),
            pltpu.SemaphoreType.DMA((3, steps)),
            pltpu.SemaphoreType.DMA(((side - 1) * side,)),
        ],
        cost_estimate=pl.CostEstimate(
            flops=4 * tokens_here * model_width * width,
            bytes_accessed=2 * model_width * (tokens_here + 2 * width),
            transcendentals=0,
        ),
        compiler_params=pltpu.CompilerParams(vmem_limit_bytes=14 << 20),
        name="kv",
    )(stay(inputs), stay(w_qkv), stay(w_out))
    w_main = [move(w, beside(m + 1)) for m, w in enumerate(w_beside)]

    earlier = []
    for s in range(1, n_seq):
        earlier.append(lax.ppermute(states, "seq", [(i, i ^ s) for i in range(n_seq)]))

    query, local, w_own, *w_rest = pl.pallas_call(
        functools.partial(q_kernel, steps=4, half_bits=half_bits, cols=cols),
        out_shape=[
            jax.ShapeDtypeStruct((tokens_here, width), BF16),
            jax.ShapeDtypeStruct((tokens_here, width), F32),
            jax.ShapeDtypeStruct((width, side * cols), BF16),
            *[jax.ShapeDtypeStruct((width, cols - early_of(cols)), BF16)] * (side - 1),
        ],
        in_specs=[VMEM, HBM, VMEM, VMEM, HBM],
        out_specs=[VMEM] * (side + 2),
        scratch_shapes=[
            scratch((model_width, width), BF16),
            scratch((tokens_here, width), F32),
            pltpu.SemaphoreType.DMA((4,)),
            pltpu.SemaphoreType.DMA((2 * side - 1,)),
        ],
        cost_estimate=pl.CostEstimate(
            flops=2 * tokens_here * model_width * width,
            bytes_accessed=2 * model_width * width,
            transcendentals=0,
        ),
        compiler_params=pltpu.CompilerParams(vmem_limit_bytes=10 << 20),
        name="qlocal",
    )(x_here, stay(w_qkv), keys, values, stay(w_out))
    w_late = [move(w, beside(m + 1)) for m, w in enumerate(w_rest)]
    w_peer = move(w_own, (1, 1))

    turn_row = turn_ids[0]
    pick_row = picked[0]
    tok_pos = jnp.arange(tokens_here, dtype=jnp.int32)
    pick_hot = tok_pos[None, :] == pick_row[:, None]
    sel_turn = jnp.sum(jnp.where(pick_hot, turn_row[None, :], 0), axis=1)
    member = (turn_row[None, :] == sel_turn[:, None]) & (tok_pos[None, :] <= pick_row[:, None])
    member = member.astype(BF16)

    ext = pl.pallas_call(
        functools.partial(attend_kernel, others=n_seq - 1),
        out_shape=jax.ShapeDtypeStruct((tokens_here, width), BF16),
        in_specs=[VMEM] * (2 + n_seq - 1),
        out_specs=VMEM,
        compiler_params=pltpu.CompilerParams(vmem_limit_bytes=4 << 20),
        name="attend",
    )(query, local, *earlier)

    ext_in = [move(ext, along(m)) for m in range(1, side)]
    ext_in_peer = [move(ext, beside(m)) for m in range(1, side)]
    ext_peer = move(ext, (1, 1))

    height = tokens_here + r_dev
    base = pl.pallas_call(
        functools.partial(here_kernel, half_bits=half_bits),
        out_shape=jax.ShapeDtypeStruct((side, height, cols), F32),
        in_specs=[VMEM] * 3 + [HBM, HBM, ANY],
        out_specs=VMEM,
        scratch_shapes=[
            scratch((height, 2 * width), BF16),
            scratch((tokens_here, cols), BF16),
            scratch((side, 2 * width, cols), BF16),
            pltpu.SemaphoreType.DMA((side + 1, 2)),
        ],
        cost_estimate=pl.CostEstimate(
            flops=4 * height * side * cols * width,
            bytes_accessed=4 * width * side * cols,
            transcendentals=0,
        ),
        compiler_params=pltpu.CompilerParams(vmem_limit_bytes=12 << 20),
        name="here",
    )(ext, ext_peer, member, stay(inputs), stay(w_out), w_peer)

    stacks = [*ext_in, *ext_in_peer]
    weights = [*w_in, *w_main]

    def project(r, kind):
        late = [] if r else w_late
        return pl.pallas_call(
            functools.partial(add_kernel, count=side - 1, r=r, rows=tokens_here),
            out_shape=[
                jax.ShapeDtypeStruct((tokens_here, cols), kind),
                jax.ShapeDtypeStruct((r_dev, cols), kind),
            ],
            in_specs=[VMEM] * (2 * len(stacks) + len(late) + 2),
            out_specs=[VMEM, VMEM],
            cost_estimate=pl.CostEstimate(
                flops=2 * height * cols * width * len(stacks),
                bytes_accessed=2 * width * cols * len(stacks),
                transcendentals=0,
            ),
            compiler_params=pltpu.CompilerParams(vmem_limit_bytes=12 << 20),
        )(*stacks, *weights, *late, member, base)

    given = [project(r, BF16) for r in range(1, side)]
    pool_in = [move(p, across(r + 1)) for r, (_, p) in enumerate(given)]
    rows_in = [move(b, across(r + 1)) for r, (b, _) in enumerate(given)]
    rows_here, pooled = project(0, F32)

    counted, pooled = lax.optimization_barrier((member, pooled))
    row_count = jnp.sum(counted.astype(F32), axis=1)
    for p in pool_in:
        pooled = pooled + p.astype(F32)
    summary = (pooled / row_count[:, None]).astype(BF16)
    summary_peer = move(summary, (1, 1))

    cap_rows = 4 * r_dev // n_head
    owner_row = owners[:, 0]
    row_pos = jnp.arange(r_dev, dtype=jnp.int32)
    head_pos = jnp.arange(n_head, dtype=jnp.int32)
    own_hot = (owner_row[:, None] == head_pos[None, :]).astype(jnp.int32)
    before = (row_pos[:, None] > row_pos[None, :]).astype(jnp.int32)
    slot_rank = jnp.sum(jnp.dot(before, own_hot) * own_hot, axis=1)
    slots = jnp.arange(cap_rows, dtype=jnp.int32)
    both = jnp.concatenate([summary, summary_peer], axis=1)
    found = []
    for j in range(chips):
        wanted = (owner_row == (head ^ (2 * j)))[None, :] & (slot_rank[None, :] == slots[:, None])
        rows = dot(wanted.astype(BF16), both).astype(BF16)
        found.append(move(rows, (2 * j, 2 * j)) if j else rows)

    mixed = pl.pallas_call(
        mix_kernel,
        out_shape=jax.ShapeDtypeStruct((tokens_here, cols), BF16),
        in_specs=[VMEM] * (1 + len(rows_in)),
        out_specs=HBM,
        scratch_shapes=[scratch((tokens_here, cols), BF16), pltpu.SemaphoreType.DMA((4,))],
        cost_estimate=pl.CostEstimate(
            flops=tokens_here * cols, bytes_accessed=8 * tokens_here * cols, transcendentals=0
        ),
        compiler_params=pltpu.CompilerParams(vmem_limit_bytes=4 << 20),
        name="mix",
    )(rows_here, *rows_in)

    def score(steps, *before):
        return pl.pallas_call(
            functools.partial(score_kernel, steps=steps, add=bool(before)),
            out_shape=jax.ShapeDtypeStruct((cap_rows, candidates.shape[0]), F32),
            in_specs=[VMEM] * (1 + len(steps) + len(before)),
            out_specs=VMEM,
            compiler_params=pltpu.CompilerParams(vmem_limit_bytes=2 << 20),
            name="score" if before else "score_first",
        )(candidates, *[found[j] for j in steps], *before)

    scores = score(range(1, chips), score(range(1)))
    return (mixed, scores)


def solution(mesh):
    return jax.shard_map(
        per_device,
        mesh=mesh,
        in_specs=(
            P("seq", None),
            P(None, None, "head"),
            P("head", None),
            P("seq", None),
            P("seq", None),
            P("seq", None),
            P(("seq", "head"), None),
        ),
        out_specs=(P("seq", "head"), P(("seq", "head"), None)),
        check_vma=False,
    )
```

```python
import functools
import jax
import jax.numpy as jnp
from jax import lax
from jax.experimental import pallas as pl
from jax.experimental.pallas import tpu as pltpu
from jax.sharding import PartitionSpec as P


HDIM = 128
F32 = jnp.float32
BF16 = jnp.bfloat16
VMEM = pl.BlockSpec(memory_space=pltpu.VMEM)
HBM = pl.BlockSpec(memory_space=pltpu.HBM)
ANY = pl.BlockSpec(memory_space=pl.ANY)


def move(value, masks):
    n = lax.axis_size("head")
    return lax.ppermute(value, "head", [(i, i ^ masks[i % 2]) for i in range(n)])


def dot(a, b):
    return jnp.dot(a, b, preferred_element_type=F32)


def masks_of(half_bits, m):
    return (m << 1, m << (1 + half_bits))


def place(half_bits, m, r, head=None):
    head = lax.axis_index("head") if head is None else head
    a, c = masks_of(half_bits, m), masks_of(half_bits, r)[::-1]
    return head ^ jnp.where(lax.bitwise_and(head, 1) == 0, a[0] ^ c[0], a[1] ^ c[1])


def block_of(index, size):
    return pl.ds(pl.multiple_of(index * size, size), size)


def early_of(cols):
    return max(HDIM, cols // 4)


def cutter(w_ref, sems, cols, half_bits, partner):
    head = lax.axis_index("head")
    head = lax.bitwise_xor(head, 1) if partner else head
    copies = []

    def take(m, r, first, size, out, to):
        start = place(half_bits, m, r, head) * cols + first
        start = pl.multiple_of(start, early_of(cols))
        copies.append(
            pltpu.make_async_copy(
                w_ref.at[:, pl.ds(start, size)], out.at[:, pl.ds(to, size)], sems.at[len(copies)]
            )
        )

    return copies, take


def kv_kernel(
    x_ref, w_ref, o_ref, k_ref, v_ref, s_ref, x_buf, *refs, steps, half_bits, cols
):
    side = 1 << half_bits
    mains = refs[: side - 1]
    w_buf, acc, sems, cut_sems = refs[side - 1 :]
    depth = x_ref.shape[1] // steps
    copies = []
    for s in range(steps):
        at = pl.ds(s * depth, depth)
        copies.append(
            [pltpu.make_async_copy(x_ref.at[:, at], x_buf.at[:, at], sems.at[0, s])]
            + [
                pltpu.make_async_copy(w_ref.at[1 + i, at], w_buf.at[i, at], sems.at[1 + i, s])
                for i in range(2)
            ]
        )
    cut, take = cutter(o_ref, cut_sems, cols, half_bits, True)
    for m in range(1, side):
        for r in range(1, side):
            take(m, r, 0, cols, mains[m - 1], (r - 1) * cols)
        take(m, 0, 0, early_of(cols), mains[m - 1], (side - 1) * cols)
    for group in (*copies[:-2], cut, *copies[-2:]):
        for copy in group:
            copy.start()
    for s in range(steps):
        for copy in copies[s]:
            copy.wait()
        at = pl.ds(s * depth, depth)
        for i in range(2):
            part = dot(x_buf[:, at], w_buf[i, at])
            acc[i] = part if s == 0 else acc[i] + part
    k_ref[...] = acc[0].astype(BF16)
    v_ref[...] = acc[1].astype(BF16)
    for h in range(k_ref.shape[1] // HDIM):
        of = pl.ds(h * HDIM, HDIM)
        state = lax.dot_general(
            k_ref[:, of], v_ref[:, of], (((0,), (0,)), ((), ())), preferred_element_type=F32
        )
        s_ref[h] = state.astype(BF16)
    for copy in cut:
        copy.wait()


def q_kernel(
    x_ref, w_ref, k_ref, v_ref, o_ref, q_ref, l_ref, own_ref, *refs, steps, half_bits, cols
):
    side = 1 << half_bits
    lates = refs[: side - 1]
    w_buf, acc, sems, cut_sems = refs[side - 1 :]
    depth = x_ref.shape[1] // steps
    rows = q_ref.shape[0]
    block = min(rows, 256)
    copies = []
    for s in range(steps):
        at = pl.ds(s * depth, depth)
        copies.append(pltpu.make_async_copy(w_ref.at[0, at], w_buf.at[at], sems.at[s]))
        copies[-1].start()
    cut, take = cutter(o_ref, cut_sems, cols, half_bits, True)
    for r in range(side):
        take(0, r, 0, cols, own_ref, r * cols)
    for m in range(1, side):
        take(m, 0, early_of(cols), cols - early_of(cols), lates[m - 1], 0)
    for copy in cut:
        copy.start()
    for s in range(steps):
        copies[s].wait()
        at = pl.ds(s * depth, depth)
        for b in range(0, rows, block):
            part = dot(x_ref[pl.ds(b, block), at], w_buf[at])
            acc[pl.ds(b, block)] = part if s == 0 else acc[pl.ds(b, block)] + part
    q_ref[...] = acc[...].astype(BF16)
    for h in range(q_ref.shape[1] // HDIM):
        of = pl.ds(h * HDIM, HDIM)
        for b in range(0, rows, block):
            seen = b + block
            sc = lax.dot_general(
                q_ref[pl.ds(b, block), of],
                k_ref[pl.ds(0, seen), of],
                (((1,), (1,)), ((), ())),
                preferred_element_type=F32,
            )
            t = lax.broadcasted_iota(jnp.int32, sc.shape, 0) + b
            s = lax.broadcasted_iota(jnp.int32, sc.shape, 1)
            sc = jnp.where(t >= s, sc, 0.0).astype(BF16)
            l_ref[pl.ds(b, block), of] = dot(sc, v_ref[pl.ds(0, seen), of])
    for copy in cut:
        copy.wait()


def attend_kernel(*refs, others):
    q_ref, l_ref = refs[:2]
    states, out_ref = refs[2 : 2 + others], refs[2 + others]
    seq = lax.axis_index("seq")
    for h in range(q_ref.shape[1] // HDIM):
        of = pl.ds(h * HDIM, HDIM)
        prefix = jnp.zeros((HDIM, HDIM), F32)
        for i, state in enumerate(states):
            prefix = prefix + jnp.where((seq ^ (i + 1)) < seq, state[h].astype(F32), 0.0)
        summed = l_ref[:, of] + dot(q_ref[:, of], prefix.astype(BF16))
        scale = lax.rsqrt(jnp.mean(summed * summed, axis=-1, keepdims=True) + 1e-05)
        out_ref[:, of] = (summed * scale).astype(BF16)


def stay(x):
    return pltpu.with_memory_space_constraint(x, pltpu.HBM)


def cut_kernel(w_ref, *refs, half_bits):
    outs, sems = refs[:-1], refs[-1]
    side = 1 << half_bits
    cols = outs[0].shape[1] // side
    copies = [
        pltpu.make_async_copy(
            w_ref.at[:, block_of(place(half_bits, m + 1, r), cols)],
            out.at[:, pl.ds(r * cols, cols)],
            sems.at[m, r],
        )
        for m, out in enumerate(outs)
        for r in range(side)
    ]
    for copy in copies:
        copy.start()
    for copy in copies:
        copy.wait()


def here_kernel(own_ref, peer_ref, m_ref, x_ref, w_ref, wp_ref, out_ref, e_buf, x_buf, w_buf, sems, *, half_bits):
    side = 1 << half_bits
    cols = out_ref.shape[2]
    rows, width = m_ref.shape[1], own_ref.shape[1]
    order = list(range(1, side)) + [0]
    copies = {}
    for r in order:
        at = block_of(place(half_bits, 0, r), cols)
        copies[r] = (
            pltpu.make_async_copy(w_ref.at[:, at], w_buf.at[r, pl.ds(0, width)], sems.at[r, 0]),
            pltpu.make_async_copy(
                wp_ref.at[:, pl.ds(r * cols, cols)], w_buf.at[r, pl.ds(width, width)], sems.at[r, 1]
            ),
        )
        for copy in copies[r]:
            copy.start()
    own = pltpu.make_async_copy(
        x_ref.at[:, block_of(lax.axis_index("head"), cols)], x_buf, sems.at[side, 0]
    )
    own.start()
    for i, ref in enumerate((own_ref, peer_ref)):
        at = pl.ds(i * width, width)
        e_buf[pl.ds(0, rows), at] = ref[...]
        e_buf[pl.ds(rows, m_ref.shape[0]), at] = dot(m_ref[...], ref[...]).astype(BF16)
    block = e_buf.shape[0] // 2
    for r in order:
        for copy in copies[r]:
            copy.wait()
        for b in range(0, e_buf.shape[0], block):
            out_ref[r, pl.ds(b, block)] = dot(e_buf[pl.ds(b, block)], w_buf[r])
    own.wait()
    out_ref[0, pl.ds(0, rows)] += x_buf[...].astype(F32)
    out_ref[0, pl.ds(rows, m_ref.shape[0])] += dot(m_ref[...], x_buf[...])


def add_kernel(*refs, count, r, rows):
    ext, w = refs[: 2 * count], refs[2 * count : 4 * count]
    late, m_ref, base = refs[4 * count : -6], refs[-6], refs[-5]
    r_ref, p_ref, l_buf, l_sems = refs[-4:]
    cols = r_ref.shape[1]
    copies = [
        pltpu.make_async_copy(ref, l_buf.at[i], l_sems.at[i]) for i, ref in enumerate(late)
    ]
    for copy in copies:
        copy.start()
    pooled = [dot(m_ref[...], e[...]).astype(BF16) for e in ext]
    split = cols // 2 if r else early_of(cols)
    for first, size in ((0, split), (split, cols - split)):
        at = pl.ds(first, size)
        if first:
            for copy in copies:
                copy.wait()
        total, few = base[r, pl.ds(0, rows), at], base[r, pl.ds(rows, m_ref.shape[0]), at]
        for i in range(2 * count):
            if i < count:
                part = w[i][:, pl.ds(r * cols + first, size)]
            elif r:
                part = w[i][:, pl.ds((r - 1) * cols + first, size)]
            elif first:
                part = l_buf[i - count]
            else:
                part = w[i][:, pl.ds(w[i].shape[1] - size, size)]
            total = total + dot(ext[i][...], part)
            few = few + dot(pooled[i], part)
        p_ref[:, at] = few.astype(p_ref.dtype)
        r_ref[:, at] = total.astype(r_ref.dtype)


def mix_kernel(*refs):
    parts, out_ref, buf, sems = refs[:-3], refs[-3], refs[-2], refs[-1]
    rows = buf.shape[0] // 4
    copies = []
    for n in range(4):
        at = pl.ds(n * rows, rows)
        total = parts[0][at]
        for part in parts[1:]:
            total = total + part[at].astype(F32)
        buf[at] = total.astype(BF16)
        copies.append(pltpu.make_async_copy(buf.at[at], out_ref.at[at], sems.at[n]))
        copies[-1].start()
    for copy in copies:
        copy.wait()


def score_kernel(c_ref, *refs, steps, add):
    slots, out_ref = refs[: len(steps)], refs[-1]
    cols = slots[0].shape[1] // 2
    head = lax.axis_index("head")
    total = refs[-2][...] if add else jnp.zeros(out_ref.shape, F32)
    for j, rows in zip(steps, slots):
        for c in range(2):
            total = total + lax.dot_general(
                rows[:, pl.ds(c * cols, cols)],
                c_ref[:, block_of(head ^ (2 * j + c), cols)],
                (((1,), (1,)), ((), ())),
                preferred_element_type=F32,
            )
    out_ref[...] = total


def per_device(inputs, w_qkv, w_out, turn_ids, picked, owners, candidates):
    tokens_here, model_width = inputs.shape
    width = w_qkv.shape[2]
    heads_here = width // HDIM
    n_head = lax.axis_size("head")
    n_seq = lax.axis_size("seq")
    chips = n_head // 2
    half_bits = (chips.bit_length() - 1) // 2
    side = 1 << half_bits
    head = lax.axis_index("head")
    cols = model_width // n_head
    r_dev = picked.shape[1]
    steps = 8

    def along(m):
        return masks_of(half_bits, m)

    def across(r):
        return along(r)[::-1]

    def beside(m):
        return tuple(mask ^ 1 for mask in across(m))

    cut = pl.pallas_call(
        functools.partial(cut_kernel, half_bits=half_bits),
        out_shape=[jax.ShapeDtypeStruct((width, side * cols), BF16)] * (side - 1),
        in_specs=[HBM],
        out_specs=[VMEM] * (side - 1),
        scratch_shapes=[pltpu.SemaphoreType.DMA((side - 1, side))],
        cost_estimate=pl.CostEstimate(
            flops=0, bytes_accessed=4 * width * side * cols * (side - 1), transcendentals=0
        ),
        compiler_params=pltpu.CompilerParams(
            vmem_limit_bytes=2 * width * side * cols * (side - 1) + (1 << 20)
        ),
        name="cut",
    )(stay(w_out))
    w_in = [move(c, along(m + 1)) for m, c in enumerate(cut)]

    scratch = pltpu.VMEM
    keys, values, states, x_here, *w_beside = pl.pallas_call(
        functools.partial(kv_kernel, steps=steps, half_bits=half_bits, cols=cols),
        out_shape=[
            jax.ShapeDtypeStruct((tokens_here, width), BF16),
            jax.ShapeDtypeStruct((tokens_here, width), BF16),
            jax.ShapeDtypeStruct((heads_here, HDIM, HDIM), BF16),
            jax.ShapeDtypeStruct((tokens_here, model_width), BF16),
            *[jax.ShapeDtypeStruct((width, (side - 1) * cols + early_of(cols)), BF16)] * (side - 1),
        ],
        in_specs=[HBM] * 3,
        out_specs=[VMEM] * (side + 3),
        scratch_shapes=[
            scratch((2, model_width, width), BF16),
            scratch((2, tokens_here, width), F32),
            pltpu.SemaphoreType.DMA((3, steps)),
            pltpu.SemaphoreType.DMA(((side - 1) * side,)),
        ],
        cost_estimate=pl.CostEstimate(
            flops=4 * tokens_here * model_width * width,
            bytes_accessed=2 * model_width * (tokens_here + 2 * width),
            transcendentals=0,
        ),
        compiler_params=pltpu.CompilerParams(vmem_limit_bytes=14 << 20),
        name="kv",
    )(stay(inputs), stay(w_qkv), stay(w_out))
    w_main = [move(w, beside(m + 1)) for m, w in enumerate(w_beside)]

    earlier = []
    for s in range(1, n_seq):
        earlier.append(lax.ppermute(states, "seq", [(i, i ^ s) for i in range(n_seq)]))

    query, local, w_own, *w_rest = pl.pallas_call(
        functools.partial(q_kernel, steps=4, half_bits=half_bits, cols=cols),
        out_shape=[
            jax.ShapeDtypeStruct((tokens_here, width), BF16),
            jax.ShapeDtypeStruct((tokens_here, width), F32),
            jax.ShapeDtypeStruct((width, side * cols), BF16),
            *[jax.ShapeDtypeStruct((width, cols - early_of(cols)), BF16)] * (side - 1),
        ],
        in_specs=[VMEM, HBM, VMEM, VMEM, HBM],
        out_specs=[VMEM] * (side + 2),
        scratch_shapes=[
            scratch((model_width, width), BF16),
            scratch((tokens_here, width), F32),
            pltpu.SemaphoreType.DMA((4,)),
            pltpu.SemaphoreType.DMA((2 * side - 1,)),
        ],
        cost_estimate=pl.CostEstimate(
            flops=2 * tokens_here * model_width * width,
            bytes_accessed=2 * model_width * width,
            transcendentals=0,
        ),
        compiler_params=pltpu.CompilerParams(vmem_limit_bytes=10 << 20),
        name="qlocal",
    )(x_here, stay(w_qkv), keys, values, stay(w_out))
    w_late = [move(w, beside(m + 1)) for m, w in enumerate(w_rest)]
    w_peer = move(w_own, (1, 1))

    turn_row = turn_ids[0]
    pick_row = picked[0]
    tok_pos = jnp.arange(tokens_here, dtype=jnp.int32)
    pick_hot = tok_pos[None, :] == pick_row[:, None]
    sel_turn = jnp.sum(jnp.where(pick_hot, turn_row[None, :], 0), axis=1)
    member = (turn_row[None, :] == sel_turn[:, None]) & (tok_pos[None, :] <= pick_row[:, None])
    member = member.astype(BF16)

    ext = pl.pallas_call(
        functools.partial(attend_kernel, others=n_seq - 1),
        out_shape=jax.ShapeDtypeStruct((tokens_here, width), BF16),
        in_specs=[VMEM] * (2 + n_seq - 1),
        out_specs=VMEM,
        compiler_params=pltpu.CompilerParams(vmem_limit_bytes=4 << 20),
        name="attend",
    )(query, local, *earlier)

    ext_in = [move(ext, along(m)) for m in range(1, side)]
    ext_in_peer = [move(ext, beside(m)) for m in range(1, side)]
    ext_peer = move(ext, (1, 1))

    height = tokens_here + r_dev
    base = pl.pallas_call(
        functools.partial(here_kernel, half_bits=half_bits),
        out_shape=jax.ShapeDtypeStruct((side, height, cols), F32),
        in_specs=[VMEM] * 3 + [HBM, HBM, ANY],
        out_specs=VMEM,
        scratch_shapes=[
            scratch((height, 2 * width), BF16),
            scratch((tokens_here, cols), BF16),
            scratch((side, 2 * width, cols), BF16),
            pltpu.SemaphoreType.DMA((side + 1, 2)),
        ],
        cost_estimate=pl.CostEstimate(
            flops=4 * height * side * cols * width,
            bytes_accessed=4 * width * side * cols,
            transcendentals=0,
        ),
        compiler_params=pltpu.CompilerParams(vmem_limit_bytes=12 << 20),
        name="here",
    )(ext, ext_peer, member, stay(inputs), stay(w_out), w_peer)

    stacks = [*ext_in, *ext_in_peer]
    weights = [*w_in, *w_main]

    def project(r, kind):
        late = [] if r else w_late
        return pl.pallas_call(
            functools.partial(add_kernel, count=side - 1, r=r, rows=tokens_here),
            out_shape=[
                jax.ShapeDtypeStruct((tokens_here, cols), kind),
                jax.ShapeDtypeStruct((r_dev, cols), kind),
            ],
            in_specs=[VMEM] * (2 * len(stacks)) + [HBM] * len(late) + [VMEM] * 2,
            out_specs=[VMEM, VMEM],
            scratch_shapes=[
                scratch((side - 1, width, cols - early_of(cols)), BF16),
                pltpu.SemaphoreType.DMA((side - 1,)),
            ],
            cost_estimate=pl.CostEstimate(
                flops=2 * height * cols * width * len(stacks),
                bytes_accessed=2 * width * cols * len(stacks),
                transcendentals=0,
            ),
            compiler_params=pltpu.CompilerParams(vmem_limit_bytes=12 << 20),
        )(*stacks, *weights, *[stay(w) for w in late], member, base)

    given = [project(r, BF16) for r in range(1, side)]
    pool_in = [move(p, across(r + 1)) for r, (_, p) in enumerate(given)]
    rows_in = [move(b, across(r + 1)) for r, (b, _) in enumerate(given)]
    rows_here, pooled = project(0, F32)

    counted, pooled = lax.optimization_barrier((member, pooled))
    row_count = jnp.sum(counted.astype(F32), axis=1)
    for p in pool_in:
        pooled = pooled + p.astype(F32)
    summary = (pooled / row_count[:, None]).astype(BF16)
    summary_peer = move(summary, (1, 1))

    cap_rows = 4 * r_dev // n_head
    owner_row = owners[:, 0]
    row_pos = jnp.arange(r_dev, dtype=jnp.int32)
    head_pos = jnp.arange(n_head, dtype=jnp.int32)
    own_hot = (owner_row[:, None] == head_pos[None, :]).astype(jnp.int32)
    before = (row_pos[:, None] > row_pos[None, :]).astype(jnp.int32)
    slot_rank = jnp.sum(jnp.dot(before, own_hot) * own_hot, axis=1)
    slots = jnp.arange(cap_rows, dtype=jnp.int32)
    both = jnp.concatenate([summary, summary_peer], axis=1)
    found = []
    for j in range(chips):
        wanted = (owner_row == (head ^ (2 * j)))[None, :] & (slot_rank[None, :] == slots[:, None])
        rows = dot(wanted.astype(BF16), both).astype(BF16)
        found.append(move(rows, (2 * j, 2 * j)) if j else rows)

    mixed = pl.pallas_call(
        mix_kernel,
        out_shape=jax.ShapeDtypeStruct((tokens_here, cols), BF16),
        in_specs=[VMEM] * (1 + len(rows_in)),
        out_specs=HBM,
        scratch_shapes=[scratch((tokens_here, cols), BF16), pltpu.SemaphoreType.DMA((4,))],
        cost_estimate=pl.CostEstimate(
            flops=tokens_here * cols, bytes_accessed=8 * tokens_here * cols, transcendentals=0
        ),
        compiler_params=pltpu.CompilerParams(vmem_limit_bytes=4 << 20),
        name="mix",
    )(rows_here, *rows_in)

    def score(steps, *before):
        return pl.pallas_call(
            functools.partial(score_kernel, steps=steps, add=bool(before)),
            out_shape=jax.ShapeDtypeStruct((cap_rows, candidates.shape[0]), F32),
            in_specs=[VMEM] * (1 + len(steps) + len(before)),
            out_specs=VMEM,
            compiler_params=pltpu.CompilerParams(vmem_limit_bytes=2 << 20),
            name="score" if before else "score_first",
        )(candidates, *[found[j] for j in steps], *before)

    scores = score(range(1, chips), score(range(1)))
    return (mixed, scores)


def solution(mesh):
    return jax.shard_map(
        per_device,
        mesh=mesh,
        in_specs=(
            P("seq", None),
            P(None, None, "head"),
            P("head", None),
            P("seq", None),
            P("seq", None),
            P("seq", None),
            P(("seq", "head"), None),
        ),
        out_specs=(P("seq", "head"), P(("seq", "head"), None)),
        check_vma=False,
    )
```
